32 devices in a mesh: groups: 2 (over x), frame: 16 (over z, y, core).
Axes of the slice: x: 2, y: 2, z: 4, core: 2. Of those that a mesh axis runs over, the one named last changes fastest.
Arguments:
- query_in: bfloat16 [32, 512, 1536], P(('groups', 'frame')), parts along dimension 0, may hold values from -200 to 200, as said below
- keys_in: bfloat16 [32, 512, 1536], P(('groups', 'frame')), parts along dimension 0, may hold values from -7 to 7, as said below
- values_in: bfloat16 [32, 512, 1536], P(('groups', 'frame')), parts along dimension 0, may hold values from -6 to 6
- far_picks: int32 [32, 6], P('groups'), parts along dimension 0, may hold values from 0 to 3
- win_rows: int32 [32], P(('groups', 'frame')), parts along dimension 0, may hold values from 1 to 15, as said below
Outputs:
- attended: bfloat16 [32, 512, 1536], P(('groups', 'frame')), parts along dimension 0
The draws below stay inside these ranges and needn't reach their ends.
There are 2 independent parts, one for each index of `groups`. The reference program is written for one: setup_inputs(seed, part) draws one part's arguments, and reference() takes and returns one part's arrays. A program takes and returns all parts, laid end to end along the dimension named above; each array names one. Nothing has to cross between parts.
Inputs may be any that keep to these rules, and one draw needn't show every extreme that they name: `query_in`: entries of the queries lie within this range. `keys_in`: entries of the keys lie within this range. `win_rows`: every draw has a frame with window 1 and a frame with window 16 - 1.
All inputs are finite; a program needn't handle non-finite values.
Results may differ from the reference program's by a relative error of at most 0.0032.
Values may be sent and summed in bfloat16 or wider, within the bound.
No kernel may reach another device: no remote copies, remote signals or barrier semaphores. Data moves between devices by JAX's collectives and lax.ppermute only.
A program may use at most 128 MiB of HBM per device.

```python
import math
import jax
import jax.numpy as jnp
from jax import lax

HD = 128
ROWS = 16
COLS = 32
SUB = 128
NREACH = 3
WIDTH = 1536
TOK = 512
FRAMES = 16
NFAR = 6


def paired_fields(key):
    first_key = jax.random.fold_in(key, 11)
    second_key = jax.random.fold_in(key, 12)
    shape = (FRAMES, TOK, WIDTH)
    keys_field = jax.random.truncated_normal(first_key, -6.0, 6.0, shape, jnp.float32)
    query_field = 2.5 * jax.random.truncated_normal(second_key, -6.0, 6.0, shape, jnp.float32)
    return (query_field, keys_field)


def draw_query_in(key, part):
    return paired_fields(key)[0].astype(jnp.bfloat16)


def draw_keys_in(key, part):
    return paired_fields(key)[1].astype(jnp.bfloat16)


def draw_win_rows(key, part):
    first_key = jax.random.fold_in(key, 21)
    second_key = jax.random.fold_in(key, 22)
    third_key = jax.random.fold_in(key, 23)
    windows = jax.random.randint(first_key, (FRAMES,), 1, ROWS, jnp.int32)
    low_spot = jax.random.randint(second_key, (), 0, FRAMES, jnp.int32)
    high_spot = (low_spot + 1 + jax.random.randint(third_key, (), 0, FRAMES - 1, jnp.int32)) % FRAMES
    windows = windows.at[low_spot].set(1)
    windows = windows.at[high_spot].set(ROWS - 1)
    return windows


def plant(values, rng, low, top_value):
    longest = values.shape.index(max(values.shape))
    spots = []
    for shift in (0, 1):
        where = [jax.random.randint(jax.random.fold_in(rng, axis), (), 0, length) for axis, length in enumerate(values.shape)]
        where[longest] = (where[longest] + shift) % values.shape[longest]
        spots.append(tuple(where))
    return values.at[spots[0]].set(low).at[spots[1]].set(top_value)


def levels(key, shape, pieces, least, top_value):
    gain, own = 1.0, jax.random.fold_in(key, 6)
    for dim, parts in pieces:
        heights = jnp.exp(jax.random.uniform(jax.random.fold_in(own, dim), (parts,), jnp.float32, least / len(pieces), top_value / len(pieces)))
        gain = gain * jnp.repeat(heights, shape[dim] // parts).reshape([-1 if axis == dim else 1 for axis in range(len(shape))])
    return gain


def noise(own_key, extent, width, bound, split=(), kind=jnp.bfloat16):
    drawn = width * jax.random.normal(own_key, extent, jnp.float32)
    if split:
        drawn = drawn * levels(own_key, extent, split, -0.22, 0.18)
    return jnp.clip(drawn, -bound, bound).astype(kind)


def setup_inputs(seed: int = 0, part: int = 0) -> dict:
    key_list = jax.random.split(jax.random.key(seed), 6)
    own_keys = jax.random.split(jax.random.fold_in(key_list[5], part), 6)
    return {
        "query_in": draw_query_in(jax.random.fold_in(jax.random.fold_in(key_list[5], part), 71), part),
        "keys_in": draw_keys_in(jax.random.fold_in(jax.random.fold_in(key_list[5], part), 71), part),
        "values_in": noise(own_keys[2], (FRAMES, TOK, WIDTH), 1.0, 6.0, ((0, 16),)),
        "far_picks": plant(jax.random.randint(own_keys[3], (FRAMES, NFAR), 0, TOK // SUB), jax.random.fold_in(own_keys[3], 1), 0, (TOK // SUB) - 1).astype(jnp.int32),
        "win_rows": draw_win_rows(jax.random.fold_in(jax.random.fold_in(key_list[5], part), 71), part),
    }


def offsets_for(frames):
    spacing = [frames // 2 ** (NREACH - level_index) for level_index in range(NREACH)]
    return [-stride for stride in spacing] + [stride for stride in spacing]

def build_mask(window, frame_ok, far_ok, tokens_count):
    query_rows = jnp.arange(tokens_count, dtype=jnp.int32) // COLS
    key_rows = jnp.tile(query_rows, 3)
    nearby = jnp.abs(query_rows[:, None] - key_rows[None, :]) <= window
    nearby = nearby & jnp.repeat(frame_ok, tokens_count)[None, :]
    distant = jnp.repeat(far_ok, SUB)[None, :]
    distant = jnp.broadcast_to(distant, (tokens_count, distant.shape[1]))
    return jnp.concatenate([nearby, distant], axis=1)

def attend(queries, key_value, allowed):
    tokens_count = queries.shape[0]
    model_width = queries.shape[1]
    heads_count = model_width // HD

    def split_heads(matrix):
        return matrix.reshape(matrix.shape[0], heads_count, HD).transpose(1, 0, 2)
    query_heads = split_heads(queries)
    key_heads = split_heads(key_value[:, :model_width])
    value_heads = split_heads(key_value[:, model_width:])

    def one_head(operands):
        query_head, key_head, value_head = operands
        scores = lax.dot_general(query_head, key_head, (((1,), (1,)), ((), ())), preferred_element_type=jnp.float32)
        scores = scores * (1.0 / math.sqrt(HD))
        scores = jnp.where(allowed, scores, -1e+30)
        row_peak = lax.optimization_barrier(jnp.max(scores, axis=1, keepdims=True))
        raw_weights = jnp.exp(scores - row_peak)
        row_total = lax.optimization_barrier(jnp.sum(raw_weights, axis=1, keepdims=True))
        weighted = jnp.dot(raw_weights.astype(jnp.bfloat16), value_head, preferred_element_type=jnp.float32)
        return weighted / row_total
    heads_out = lax.map(one_head, (query_heads, key_heads, value_heads))
    return heads_out.transpose(1, 0, 2).reshape(tokens_count, model_width).astype(jnp.bfloat16)

def reference(query_in, keys_in, values_in, far_picks, win_rows):
    key_value = jnp.concatenate([keys_in, values_in], axis=2)
    tokens_count = key_value.shape[1]
    double_width = key_value.shape[2]
    padded = jnp.pad(key_value, ((1, 1), (0, 0), (0, 0)))
    offset_list = jnp.array(offsets_for(FRAMES), dtype=jnp.int32)

    def one_frame(position):
        beside_all = lax.dynamic_slice_in_dim(padded, position, 3, 0).reshape(3 * tokens_count, double_width)
        sources = jnp.clip(position + offset_list, 0, FRAMES - 1).astype(jnp.int32)
        picks_row = far_picks[position].astype(jnp.int32)

        def take_block(source, picked):
            start = (picked * SUB).astype(jnp.int32)
            return lax.dynamic_slice(key_value, (source, start, jnp.int32(0)), (1, SUB, double_width))[0]
        distant = jax.vmap(take_block)(sources, picks_row).reshape(offset_list.shape[0] * SUB, double_width)
        frame_ok = jnp.stack([position >= 1, position >= 0, position + 1 < FRAMES])
        far_ok = (position + offset_list >= 0) & (position + offset_list < FRAMES)
        allowed = build_mask(win_rows[position], frame_ok, far_ok, tokens_count)
        key_all = jnp.concatenate([beside_all, distant], axis=0)
        return attend(query_in[position], key_all, allowed)
    return lax.map(one_frame, jnp.arange(FRAMES, dtype=jnp.int32))
```

```python
import functools
import math

import jax
import jax.numpy as jnp
from jax import lax
from jax.experimental import pallas as pl
from jax.experimental.pallas import tpu as pltpu
from jax.sharding import PartitionSpec as P

HD = 128
COLS = 32
SUB = 128
NREACH = 3
MASKED = -1e30
BASE2 = math.log2(math.e) / math.sqrt(HD)
QUERY_BLOCK = 128


def offsets_for(frames):
    spacing = [frames // 2 ** (NREACH - level_index) for level_index in range(NREACH)]
    return [-stride for stride in spacing] + [stride for stride in spacing]


def shifted(value, steps):
    count = lax.axis_size("frame")
    pairs = [(i, i + steps) for i in range(count) if 0 <= i + steps < count]
    return lax.ppermute(value, "frame", pairs)


def attend_kernel(kinds, first, last, flags_ref, q_ref, *refs):
    count = len(kinds)
    sources = [(refs[2 * i], refs[2 * i + 1]) for i in range(count)]
    refs = refs[2 * count :]
    if not first:
        acc_in, stat_in = refs[:2]
        refs = refs[2:]
    if last:
        (out_ref,) = refs[:1]
        refs = refs[1:]
    else:
        acc_out, stat_out = refs[:2]
        refs = refs[2:]
    tokens = q_ref.shape[0]
    windowed = [i for i in range(count) if kinds[i]]
    if windowed:
        bias_ref, hot_ref = refs

        @pl.when(pl.program_id(0) == 0)
        def _():
            row = lax.broadcasted_iota(jnp.int32, (tokens, HD), 0) // COLS
            lane = lax.broadcasted_iota(jnp.int32, (tokens, HD), 1)
            hot_ref[...] = jnp.where(row == lane, 1.0, 0.0).astype(jnp.bfloat16)
            for slot, i in enumerate(windowed):
                near = jnp.abs(row - lane) <= flags_ref[i]
                bias_ref[slot] = jnp.where(near, 0.0, MASKED).astype(jnp.bfloat16)

    for start in range(0, tokens, QUERY_BLOCK):
        rows = pl.ds(start, QUERY_BLOCK)
        query = q_ref[rows, :]
        scores = []
        if first:
            peak = jnp.full((QUERY_BLOCK, 1), MASKED, jnp.float32)
        else:
            before = stat_in[rows, 0:1]
            peak = before
        for i, (key_ref, _) in enumerate(sources):
            lhs, rhs = query, key_ref[...]
            if kinds[i]:
                lhs = jnp.concatenate([lhs, bias_ref[windowed.index(i), rows, :]], axis=1)
                rhs = jnp.concatenate([rhs, hot_ref[...]], axis=1)
            score = lax.dot_general(
                lhs, rhs, (((1,), (1,)), ((), ())), preferred_element_type=jnp.float32
            )
            top = jnp.max(score, axis=1, keepdims=True)
            if not kinds[i]:
                top = jnp.where(flags_ref[i] > 0, top, MASKED)
            peak = jnp.maximum(peak, top)
            scores.append(score)
        total = None
        for i, (_, value_ref) in enumerate(sources):
            level = peak if kinds[i] else jnp.where(flags_ref[i] > 0, peak, -MASKED)
            weights = jnp.exp2((scores[i] - level) * BASE2).astype(jnp.bfloat16)
            values = jnp.concatenate(
                [value_ref[...], jnp.ones((value_ref.shape[0], HD), jnp.bfloat16)], axis=1
            )
            part = jnp.dot(weights, values, preferred_element_type=jnp.float32)
            total = part if total is None else total + part
        acc, norm = total[:, :HD], total[:, HD:]
        if not first:
            scale = jnp.exp2((before - peak) * BASE2)
            acc = acc + acc_in[rows, :] * scale
            norm = norm + stat_in[rows, HD // 2 : HD // 2 + 1] * scale
        if last:
            out_ref[rows, :] = (acc / norm).astype(out_ref.dtype)
        else:
            acc_out[rows, :] = acc
            lane = lax.broadcasted_iota(jnp.int32, (QUERY_BLOCK, HD), 1)
            stat_out[rows, :] = jnp.where(lane < HD // 2, peak, norm)


def attend(query, sources, state, last):
    tokens, width = query.shape
    heads = width // HD
    kinds = tuple(source[4] for source in sources)
    flags = jnp.stack([jnp.asarray(source[5], jnp.int32) for source in sources])

    def column(rows, base):
        return pl.BlockSpec((rows, HD), lambda h, flags: (0, base + h))

    specs, operands = [column(tokens, 0)], [query]
    keys_count = 0
    for key, key_base, value, value_base, _, _ in sources:
        specs += [column(key.shape[0], key_base), column(key.shape[0], value_base)]
        operands += [key, value]
        keys_count += key.shape[0]
    if state is not None:
        specs += [column(tokens, 0)] * 2
        operands += list(state)
    if last:
        out_shape = jax.ShapeDtypeStruct((tokens, width), jnp.bfloat16)
        out_specs = column(tokens, 0)
    else:
        out_shape = [jax.ShapeDtypeStruct((tokens, width), jnp.float32)] * 2
        out_specs = [column(tokens, 0)] * 2
    scratch = []
    if any(kinds):
        scratch = [
            pltpu.VMEM((sum(kinds), tokens, HD), jnp.bfloat16),
            pltpu.VMEM((tokens, HD), jnp.bfloat16),
        ]
    return pl.pallas_call(
        functools.partial(attend_kernel, kinds, state is None, last),
        out_shape=out_shape,
        grid_spec=pltpu.PrefetchScalarGridSpec(
            num_scalar_prefetch=1,
            grid=(heads,),
            in_specs=specs,
            out_specs=out_specs,
            scratch_shapes=scratch,
        ),
        compiler_params=pltpu.CompilerParams(vmem_limit_bytes=32 << 20),
        cost_estimate=pl.CostEstimate(
            flops=4 * tokens * keys_count * width,
            bytes_accessed=2 * (tokens + 2 * keys_count) * width + 8 * tokens * width,
            transcendentals=tokens * keys_count * heads,
        ),
    )(flags, *operands)


def body(query_in, keys_in, values_in, far_picks, win_rows):
    frames = lax.axis_size("frame")
    position = lax.axis_index("frame")
    query, keys, values = query_in[0], keys_in[0], values_in[0]
    heads = query.shape[1] // HD
    window = win_rows[0]
    offsets = offsets_for(frames)
    even = position % 2 == 0
    partner = position + 1 - 2 * (position % 2)
    shared = frames % 2 == 0 and 2 in offsets
    back, ahead = (offsets.index(-2), offsets.index(2)) if shared else (None, None)

    def block_for(reader, column, keys, values):
        reader = jnp.clip(reader, 0, frames - 1)
        pick = far_picks[reader, column] * SUB
        return jnp.concatenate(
            [
                lax.dynamic_slice_in_dim(keys, pick, SUB, 0),
                lax.dynamic_slice_in_dim(values, pick, SUB, 0),
            ],
            axis=1,
        )

    def there(frame):
        return ((frame >= 0) & (frame < frames)).astype(jnp.int32)

    far = []
    for column in sorted(range(len(offsets)), key=lambda c: -abs(offsets[c])):
        offset = offsets[column]
        if shared and abs(offset) == 2:
            continue
        chosen = block_for(position - offset, column, keys, values)
        far.append((shifted(chosen, -offset), there(position + offset)))
    key_value = jnp.concatenate([keys, values], axis=1)
    across = [(i, i + 1) for i in range(1, frames - 1, 2)]
    across += [(i + 1, i) for i in range(1, frames - 1, 2)]
    beyond = lax.ppermute(key_value, "frame", across)
    beyond_there = there(position + jnp.where(even, -1, 1))
    if shared:
        reader = position + jnp.where(even, 2, -2)
        chosen = block_for(reader, jnp.where(even, back, ahead), keys, values)
        pairs = [(i, i + 2) for i in range(0, frames - 2, 2)]
        pairs += [(i, i - 2) for i in range(3, frames, 2)]
        far.append((lax.ppermute(chosen, "frame", pairs), there(position + jnp.where(even, -2, 2))))
    swap = [(i, i ^ 1) for i in range(frames)]
    beside = lax.ppermute(key_value, "frame", swap)

    state = attend(
        query,
        [(keys, 0, values, 0, True, window), (beside, 0, beside, heads, True, window)],
        None,
        False,
    )
    state = attend(
        query, [(piece, 0, piece, heads, False, flag) for piece, flag in far], state, False
    )
    rest = [(beyond, 0, beyond, heads, True, jnp.where(beyond_there > 0, window, -1))]
    if shared:
        column = jnp.where(even, back, ahead)
        chosen = block_for(partner, column, beyond[:, : keys.shape[1]], beyond[:, keys.shape[1] :])
        relayed = lax.ppermute(chosen, "frame", swap)
        rest.append((relayed, 0, relayed, heads, False, there(position + jnp.where(even, 2, -2))))
    return attend(query, rest, state, True)[None]


def solution(mesh):
    in_specs = (
        P(("groups", "frame"), None, None),
        P(("groups", "frame"), None, None),
        P(("groups", "frame"), None, None),
        P("groups", None),
        P(("groups", "frame")),
    )
    out_specs = P(("groups", "frame"), None, None)
    return jax.shard_map(body, mesh=mesh, in_specs=in_specs, out_specs=out_specs, check_vma=False)
```

```python
import functools
import math

import jax
import jax.numpy as jnp
from jax import lax
from jax.experimental import pallas as pl
from jax.experimental.pallas import tpu as pltpu
from jax.sharding import PartitionSpec as P

HD = 128
COLS = 32
SUB = 128
NREACH = 3
MASKED = -1e30
BASE2 = math.log2(math.e) / math.sqrt(HD)
QUERY_BLOCK = 256


def offsets_for(frames):
    spacing = [frames // 2 ** (NREACH - level_index) for level_index in range(NREACH)]
    return [-stride for stride in spacing] + [stride for stride in spacing]


def shifted(value, steps):
    count = lax.axis_size("frame")
    pairs = [(i, i + steps) for i in range(count) if 0 <= i + steps < count]
    return lax.ppermute(value, "frame", pairs)


def attend_kernel(kinds, first, last, flags_ref, q_ref, *refs):
    count = len(kinds)
    sources = [(refs[2 * i], refs[2 * i + 1]) for i in range(count)]
    refs = refs[2 * count :]
    if not first:
        acc_in, stat_in = refs[:2]
        refs = refs[2:]
    if last:
        out_ref, bias_ref, class_ref = refs
    else:
        acc_out, stat_out, bias_ref, class_ref = refs
    tokens = q_ref.shape[0]

    @pl.when(pl.program_id(0) == 0)
    def _():
        lane = lax.broadcasted_iota(jnp.int32, (tokens, HD), 1)
        row = lax.broadcasted_iota(jnp.int32, (tokens, HD), 0) // COLS
        bias = jnp.zeros((tokens, HD), jnp.float32)
        base, start = 0, 0
        for i, (key_ref, _) in enumerate(sources):
            size = key_ref.shape[0]
            if kinds[i]:
                wide = size // COLS
                here = jnp.abs(row - (lane - base)) <= flags_ref[i]
                hot = row == lane - base
            else:
                wide = 1
                here = lane * 0 + flags_ref[i] > 0
                hot = lane == base
            mine = (lane >= base) & (lane < base + wide)
            bias = jnp.where(mine & ~here, MASKED, bias)
            class_ref[pl.ds(start, size), :] = jnp.where(hot, 1.0, 0.0).astype(jnp.bfloat16)[:size]
            base, start = base + wide, start + size
        bias_ref[...] = bias.astype(jnp.bfloat16)

    keys = jnp.concatenate([key_ref[...] for key_ref, _ in sources], axis=0)
    values = jnp.concatenate([value_ref[...] for _, value_ref in sources], axis=0)
    keys = jnp.concatenate([keys, class_ref[...]], axis=1)
    values = jnp.concatenate([values, jnp.ones_like(values)], axis=1)
    for start in range(0, tokens, QUERY_BLOCK):
        rows = pl.ds(start, QUERY_BLOCK)
        query = jnp.concatenate([q_ref[rows, :], bias_ref[rows, :]], axis=1)
        score = lax.dot_general(
            query, keys, (((1,), (1,)), ((), ())), preferred_element_type=jnp.float32
        )
        peak = jnp.max(score, axis=1, keepdims=True)
        if not first:
            before = stat_in[rows, 0:1]
            peak = jnp.maximum(peak, before)
        weights = jnp.exp2((score - peak) * BASE2).astype(jnp.bfloat16)
        total = jnp.dot(weights, values, preferred_element_type=jnp.float32)
        acc, norm = total[:, :HD], total[:, HD:]
        if not first:
            scale = jnp.exp2((before - peak) * BASE2)
            acc = acc + acc_in[rows, :] * scale
            norm = norm + stat_in[rows, HD // 2 : HD // 2 + 1] * scale
        if last:
            out_ref[rows, :] = (acc / norm).astype(out_ref.dtype)
        else:
            acc_out[rows, :] = acc
            lane = lax.broadcasted_iota(jnp.int32, (QUERY_BLOCK, HD), 1)
            stat_out[rows, :] = jnp.where(lane < HD // 2, peak, norm)


def attend(query, sources, state, last):
    tokens, width = query.shape
    heads = width // HD
    kinds = tuple(source[4] for source in sources)
    flags = jnp.stack([jnp.asarray(source[5], jnp.int32) for source in sources])

    def column(rows, base):
        return pl.BlockSpec((rows, HD), lambda h, flags: (0, base + h))

    specs, operands = [column(tokens, 0)], [query]
    keys_count = 0
    for key, key_base, value, value_base, _, _ in sources:
        specs += [column(key.shape[0], key_base), column(key.shape[0], value_base)]
        operands += [key, value]
        keys_count += key.shape[0]
    if state is not None:
        specs += [column(tokens, 0)] * 2
        operands += list(state)
    if last:
        out_shape = jax.ShapeDtypeStruct((tokens, width), jnp.bfloat16)
        out_specs = column(tokens, 0)
    else:
        out_shape = [jax.ShapeDtypeStruct((tokens, width), jnp.float32)] * 2
        out_specs = [column(tokens, 0)] * 2
    return pl.pallas_call(
        functools.partial(attend_kernel, kinds, state is None, last),
        out_shape=out_shape,
        grid_spec=pltpu.PrefetchScalarGridSpec(
            num_scalar_prefetch=1,
            grid=(heads,),
            in_specs=specs,
            out_specs=out_specs,
            scratch_shapes=[
                pltpu.VMEM((tokens, HD), jnp.bfloat16),
                pltpu.VMEM((keys_count, HD), jnp.bfloat16),
            ],
        ),
        compiler_params=pltpu.CompilerParams(vmem_limit_bytes=60 << 20),
        cost_estimate=pl.CostEstimate(
            flops=4 * tokens * keys_count * width,
            bytes_accessed=2 * (tokens + 2 * keys_count) * width + 8 * tokens * width,
            transcendentals=tokens * keys_count * heads,
        ),
    )(flags, *operands)


def body(query_in, keys_in, values_in, far_picks, win_rows):
    frames = lax.axis_size("frame")
    position = lax.axis_index("frame")
    query, keys, values = query_in[0], keys_in[0], values_in[0]
    heads = query.shape[1] // HD
    window = win_rows[0]
    offsets = offsets_for(frames)
    even = position % 2 == 0
    partner = position + 1 - 2 * (position % 2)
    shared = frames % 2 == 0 and 2 in offsets
    back, ahead = (offsets.index(-2), offsets.index(2)) if shared else (None, None)

    def block_for(reader, column, keys, values):
        reader = jnp.clip(reader, 0, frames - 1)
        pick = far_picks[reader, column] * SUB
        return jnp.concatenate(
            [
                lax.dynamic_slice_in_dim(keys, pick, SUB, 0),
                lax.dynamic_slice_in_dim(values, pick, SUB, 0),
            ],
            axis=1,
        )

    def there(frame):
        return ((frame >= 0) & (frame < frames)).astype(jnp.int32)

    far = []
    for column in sorted(range(len(offsets)), key=lambda c: -abs(offsets[c])):
        offset = offsets[column]
        if shared and abs(offset) == 2:
            continue
        chosen = block_for(position - offset, column, keys, values)
        far.append((shifted(chosen, -offset), there(position + offset)))
    key_value = jnp.concatenate([keys, values], axis=1)
    across = [(i, i + 1) for i in range(1, frames - 1, 2)]
    across += [(i + 1, i) for i in range(1, frames - 1, 2)]
    beyond = lax.ppermute(key_value, "frame", across)
    beyond_there = there(position + jnp.where(even, -1, 1))
    if shared:
        reader = position + jnp.where(even, 2, -2)
        chosen = block_for(reader, jnp.where(even, back, ahead), keys, values)
        pairs = [(i, i + 2) for i in range(0, frames - 2, 2)]
        pairs += [(i, i - 2) for i in range(3, frames, 2)]
        far.append((lax.ppermute(chosen, "frame", pairs), there(position + jnp.where(even, -2, 2))))
    swap = [(i, i ^ 1) for i in range(frames)]
    beside = lax.ppermute(key_value, "frame", swap)

    state = attend(
        query,
        [(keys, 0, values, 0, True, window), (beside, 0, beside, heads, True, window)],
        None,
        False,
    )
    state = attend(
        query, [(piece, 0, piece, heads, False, flag) for piece, flag in far], state, False
    )
    state, beyond = lax.optimization_barrier((state, beyond))
    rest = [(beyond, 0, beyond, heads, True, jnp.where(beyond_there > 0, window, -1))]
    if shared:
        column = jnp.where(even, back, ahead)
        chosen = block_for(partner, column, beyond[:, : keys.shape[1]], beyond[:, keys.shape[1] :])
        relayed = lax.ppermute(chosen, "frame", swap)
        rest.append((relayed, 0, relayed, heads, False, there(position + jnp.where(even, 2, -2))))
    return attend(query, rest, state, True)[None]


def solution(mesh):
    in_specs = (
        P(("groups", "frame"), None, None),
        P(("groups", "frame"), None, None),
        P(("groups", "frame"), None, None),
        P("groups", None),
        P(("groups", "frame")),
    )
    out_specs = P(("groups", "frame"), None, None)
    return jax.shard_map(body, mesh=mesh, in_specs=in_specs, out_specs=out_specs, check_vma=False)
```

```python
import functools
import math

import jax
import jax.numpy as jnp
from jax import lax
from jax.experimental import pallas as pl
from jax.experimental.pallas import tpu as pltpu
from jax.sharding import PartitionSpec as P

HD = 128
COLS = 32
SUB = 128
NREACH = 3
MASKED = -1e30
BASE2 = math.log2(math.e) / math.sqrt(HD)
ONES = 16


def offsets_for(frames):
    spacing = [frames // 2 ** (NREACH - level_index) for level_index in range(NREACH)]
    return [-stride for stride in spacing] + [stride for stride in spacing]


def moved(value, steps):
    count = lax.axis_size("frame")
    pairs = [(f, f + step) for step, who in steps for f in range(count) if who(f)]
    pairs = [(source, target) for source, target in pairs if 0 <= target < count]
    return lax.ppermute(value, "frame", pairs)


def anyone(frame):
    return True


def is_even(frame):
    return frame % 2 == 0


def is_odd(frame):
    return frame % 2 == 1


def gather_kernel(readers, frames, picks_ref, keys_ref, values_ref, *refs):
    outs, sems = refs[: len(readers)], refs[len(readers)]
    width = keys_ref.shape[1]
    position = lax.axis_index("frame")
    copies = []
    for slot, (reader_of, out) in enumerate(zip(readers, outs)):
        reader, column = reader_of(position)
        pick = picks_ref[jnp.clip(reader, 0, frames - 1), column]
        rows = pl.ds(pl.multiple_of(pick * SUB, SUB), SUB)
        for half, source in enumerate((keys_ref, values_ref)):
            target = out.at[:, pl.ds(half * width, width)]
            copies.append(
                pltpu.make_async_copy(source.at[rows, :], target, sems.at[2 * slot + half])
            )
    for copy in copies:
        copy.start()
    for copy in copies:
        copy.wait()


def gather(picks, keys, values, readers, frames):
    width = keys.shape[1]
    shape = (SUB, 2 * width)
    return pl.pallas_call(
        functools.partial(gather_kernel, readers, frames),
        out_shape=[jax.ShapeDtypeStruct(shape, keys.dtype) for _ in readers],
        in_specs=[
            pl.BlockSpec(memory_space=pltpu.SMEM),
            pl.BlockSpec(memory_space=pl.ANY),
            pl.BlockSpec(memory_space=pl.ANY),
        ],
        out_specs=[pl.BlockSpec(memory_space=pltpu.VMEM) for _ in readers],
        scratch_shapes=[pltpu.SemaphoreType.DMA((2 * len(readers),))],
        compiler_params=pltpu.CompilerParams(vmem_limit_bytes=60 << 20),
        cost_estimate=pl.CostEstimate(
            flops=0, bytes_accessed=8 * SUB * width * len(readers), transcendentals=0
        ),
    )(picks, keys, values)


def attend_kernel(kinds, together, first, last, window_ref, q_ref, *refs):
    count = len(kinds)
    sources = [(refs[2 * i], refs[2 * i + 1]) for i in range(count)]
    refs = refs[2 * count :]
    if not first:
        acc_in, stat_in = refs[:2]
        refs = refs[2:]
    if last:
        out_ref, bias_ref, class_ref, turned_ref = refs
    else:
        acc_out, stat_out, bias_ref, class_ref, turned_ref = refs
    tokens = q_ref.shape[0]
    sizes = [key_ref.shape[0] for key_ref, _ in sources]

    @pl.when(pl.program_id(0) == 0)
    def _():
        position = lax.axis_index("frame")
        row = lax.broadcasted_iota(jnp.int32, (tokens, HD), 0) // COLS
        lane = lax.broadcasted_iota(jnp.int32, (tokens, HD), 1)
        bias = jnp.zeros((tokens, HD), jnp.float32)
        base, start = 0, 0
        for (windowed, there), size in zip(kinds, sizes):
            there = there(position)
            if windowed:
                wide = size // COLS
                here = jnp.abs(row - (lane - base)) <= jnp.where(there, window_ref[0], -1)
                hot = row[:size] == lane[:size] - base
            else:
                wide = 1
                here = lane * 0 + jnp.where(there, 1, 0) > 0
                hot = lane[:size] == base
            mine = (lane >= base) & (lane < base + wide)
            bias = jnp.where(mine & ~here, MASKED, bias)
            class_ref[pl.ds(start, size), :] = jnp.where(hot, 1.0, 0.0).astype(jnp.bfloat16)
            base, start = base + wide, start + size
        bias_ref[...] = bias.astype(jnp.bfloat16)
        turned_ref[:, pl.ds(HD, ONES), :] = jnp.ones((together, ONES, sum(sizes)), jnp.bfloat16)

    def column(head):
        return pl.ds(head * HD, HD)

    def scores_of(head):
        keys = jnp.concatenate([key_ref[:, column(head)] for key_ref, _ in sources], axis=0)
        keys = jnp.concatenate([keys, class_ref[...]], axis=1)
        query = jnp.concatenate([q_ref[:, column(head)], bias_ref[...]], axis=1)
        scores = lax.dot_general(
            keys, query, (((1,), (1,)), ((), ())), preferred_element_type=jnp.float32
        )
        return scores, jnp.max(scores, axis=0, keepdims=True)

    for head in range(together):
        start = 0
        for (_, value_ref), size in zip(sources, sizes):
            turned_ref[head, pl.ds(0, HD), pl.ds(start, size)] = value_ref[:, column(head)].T
            start += size
    upcoming = scores_of(0)
    for head in range(together):
        scores, peak = upcoming
        if head + 1 < together:
            upcoming = scores_of(head + 1)
        if not first:
            before = stat_in[8 * head : 8 * head + 1, :]
            peak = jnp.maximum(peak, before)
        weights = jnp.exp2((scores - peak) * BASE2).astype(jnp.bfloat16)
        total = jnp.dot(turned_ref[head], weights, preferred_element_type=jnp.float32)
        acc, norm = total[:HD, :], total[HD : HD + 1, :]
        if not first:
            scale = jnp.exp2((before - peak) * BASE2)
            acc = acc + acc_in[column(head), :] * scale
            norm = norm + stat_in[8 * head + 1 : 8 * head + 2, :] * scale
        if last:
            out_ref[:, column(head)] = (acc / norm).T.astype(out_ref.dtype)
        else:
            acc_out[column(head), :] = acc
            stat_out[8 * head : 8 * head + 1, :] = peak
            stat_out[8 * head + 1 : 8 * head + 2, :] = norm


def attend(window, query, sources, state, last):
    tokens, width = query.shape
    heads = width // HD
    together = next(n for n in (3, 2, 1) if heads % n == 0)
    kinds = tuple(source[4:] for source in sources)

    def columns(rows, base):
        return pl.BlockSpec((rows, HD * together), lambda h, window: (0, base // together + h))

    specs, operands = [columns(tokens, 0)], [query]
    keys_count = 0
    for key, key_base, value, value_base, _, _ in sources:
        specs += [columns(key.shape[0], key_base), columns(key.shape[0], value_base)]
        operands += [key, value]
        keys_count += key.shape[0]
    state_specs = [
        pl.BlockSpec((HD * together, tokens), lambda h, window: (h, 0)),
        pl.BlockSpec((8 * together, tokens), lambda h, window: (h, 0)),
    ]
    moved_bytes = 2 * (tokens + 2 * keys_count) * width
    if state is not None:
        specs += state_specs
        operands += list(state)
        moved_bytes += 4 * tokens * width
    if last:
        out_shape = jax.ShapeDtypeStruct((tokens, width), jnp.bfloat16)
        out_specs = columns(tokens, 0)
    else:
        out_shape = [
            jax.ShapeDtypeStruct((width, tokens), jnp.float32),
            jax.ShapeDtypeStruct((8 * heads, tokens), jnp.float32),
        ]
        out_specs = state_specs
    return pl.pallas_call(
        functools.partial(attend_kernel, kinds, together, state is None, last),
        out_shape=out_shape,
        grid_spec=pltpu.PrefetchScalarGridSpec(
            num_scalar_prefetch=1,
            grid=(heads // together,),
            in_specs=specs,
            out_specs=out_specs,
            scratch_shapes=[
                pltpu.VMEM((tokens, HD), jnp.bfloat16),
                pltpu.VMEM((keys_count, HD), jnp.bfloat16),
                pltpu.VMEM((together, HD + ONES, keys_count), jnp.bfloat16),
            ],
        ),
        compiler_params=pltpu.CompilerParams(vmem_limit_bytes=60 << 20),
        cost_estimate=pl.CostEstimate(
            flops=4 * tokens * keys_count * width,
            bytes_accessed=moved_bytes + 2 * tokens * width,
            transcendentals=tokens * keys_count * heads,
        ),
    )(window, *operands)


def body(query_in, keys_in, values_in, far_picks, win_rows):
    frames = lax.axis_size("frame")
    query, keys, values = query_in[0], keys_in[0], values_in[0]
    heads = query.shape[1] // HD
    offsets = offsets_for(frames)
    shared = frames % 2 == 0 and 2 in offsets

    def beyond_of(position):
        return position + 2 * (position % 2) - 1

    def there(frame):
        return (frame >= 0) & (frame < frames)

    outward = [(1, is_odd), (-1, is_even)]
    inward = [(1, is_even), (-1, is_odd)]
    beyond_keys = moved(keys, outward)
    beyond_values = moved(values, outward)
    beyond = [beyond_keys, beyond_values]

    far = []
    for column in sorted(range(len(offsets)), key=lambda c: -abs(offsets[c])):
        offset = offsets[column]
        if shared and abs(offset) == 2:
            continue
        if 2 * abs(offset) == frames:
            if offset > 0:
                continue
            back, ahead = column, offsets.index(-offset)
            half = -offset

            def across(position, half=half, back=back, ahead=ahead):
                low = position < half
                return position + jnp.where(low, half, -half), jnp.where(low, back, ahead)

            steps = [(half, lambda f, half=half: f < half), (-half, lambda f, half=half: f >= half)]
            far.append((steps, across, lambda position: position >= 0))
            continue
        far.append(
            (
                [(-offset, anyone)],
                lambda position, offset=offset, column=column: (position - offset, column),
                lambda position, offset=offset: there(position + offset),
            )
        )
    if shared:
        back, ahead = offsets.index(-2), offsets.index(2)

        def two_on(position):
            odd = position % 2
            return position + 2 - 4 * odd, jnp.where(odd == 0, back, ahead)

        def two_back(position):
            return there(position - 2 + 4 * (position % 2))

        def partner(position):
            odd = position % 2
            return position + 1 - 2 * odd, jnp.where(odd == 0, back, ahead)

        far.append(([(2, is_even), (-2, is_odd)], two_on, two_back))
    blocks = gather(far_picks, keys, values, [reader for _, reader, _ in far], frames)
    arrived = []
    for block, (steps, _, _) in zip(blocks, far):
        arrived.append(moved(block, steps))
    mate_keys = moved(keys, inward)
    mate_values = moved(values, inward)

    def always(position):
        return position >= 0

    def near_there(position):
        return there(beyond_of(position))

    own = [(keys, 0, values, 0, True, always), (mate_keys, 0, mate_values, 0, True, always)]
    state = attend(win_rows, query, own, None, False)
    nearby = [(beyond[0], 0, beyond[1], 0, True, near_there)]
    if shared:
        (handed,) = gather(far_picks, *beyond, [partner], frames)
        handed = moved(handed, inward)
        nearby.append(
            (handed, 0, handed, heads, False, lambda p: there(p + 2 - 4 * (p % 2)))
        )
    state = attend(win_rows, query, nearby, state, False)
    distant = [
        (block, 0, block, heads, False, there) for block, (_, _, there) in zip(arrived, far)
    ]
    return attend(win_rows, query, distant, state, True)[None]


def solution(mesh):
    in_specs = (
        P(("groups", "frame"), None, None),
        P(("groups", "frame"), None, None),
        P(("groups", "frame"), None, None),
        P("groups", None),
        P(("groups", "frame")),
    )
    out_specs = P(("groups", "frame"), None, None)

    return jax.shard_map(body, mesh=mesh, in_specs=in_specs, out_specs=out_specs, check_vma=False)
```

```python
import functools
import math

import jax
import jax.numpy as jnp
from jax import lax
from jax.experimental import pallas as pl
from jax.experimental.pallas import tpu as pltpu
from jax.sharding import PartitionSpec as P

HD = 128
COLS = 32
SUB = 128
NREACH = 3
MASKED = -1e30
BASE2 = math.log2(math.e) / math.sqrt(HD)
ONES = 16


def offsets_for(frames):
    spacing = [frames // 2 ** (NREACH - level_index) for level_index in range(NREACH)]
    return [-stride for stride in spacing] + [stride for stride in spacing]


def moved(value, steps):
    count = lax.axis_size("frame")
    pairs = [(f, f + step) for step, who in steps for f in range(count) if who(f)]
    pairs = [(source, target) for source, target in pairs if 0 <= target < count]
    return lax.ppermute(value, "frame", pairs)


def anyone(frame):
    return True


def is_even(frame):
    return frame % 2 == 0


def is_odd(frame):
    return frame % 2 == 1


def gather_kernel(readers, frames, picks_ref, keys_ref, values_ref, *refs):
    outs, sems = refs[: len(readers)], refs[len(readers)]
    width = keys_ref.shape[1]
    position = lax.axis_index("frame")
    copies = []
    for slot, (reader_of, out) in enumerate(zip(readers, outs)):
        reader, column = reader_of(position)
        pick = picks_ref[column, jnp.clip(reader, 0, frames - 1)]
        rows = pl.ds(pl.multiple_of(pick * SUB, SUB), SUB)
        for half, source in enumerate((keys_ref, values_ref)):
            target = out.at[:, pl.ds(half * width, width)]
            copies.append(
                pltpu.make_async_copy(source.at[rows, :], target, sems.at[2 * slot + half])
            )
    for copy in copies:
        copy.start()
    for copy in copies:
        copy.wait()


def gather(picks, keys, values, readers, frames):
    width = keys.shape[1]
    shape = (SUB, 2 * width)
    return pl.pallas_call(
        functools.partial(gather_kernel, readers, frames),
        out_shape=[jax.ShapeDtypeStruct(shape, keys.dtype) for _ in readers],
        in_specs=[
            pl.BlockSpec(memory_space=pltpu.SMEM),
            pl.BlockSpec(memory_space=pltpu.HBM),
            pl.BlockSpec(memory_space=pltpu.HBM),
        ],
        out_specs=[pl.BlockSpec(memory_space=pltpu.VMEM) for _ in readers],
        scratch_shapes=[pltpu.SemaphoreType.DMA((2 * len(readers),))],
        compiler_params=pltpu.CompilerParams(vmem_limit_bytes=67_043_328),
        cost_estimate=pl.CostEstimate(
            flops=0, bytes_accessed=8 * SUB * width * len(readers), transcendentals=0
        ),
    )(picks.T, keys, values)


def attend_kernel(kinds, together, first, last, window_ref, q_ref, *refs):
    count = len(kinds)
    sources = [(refs[2 * i], refs[2 * i + 1]) for i in range(count)]
    refs = refs[2 * count :]
    if not first:
        acc_in, stat_in = refs[:2]
        refs = refs[2:]
    if last:
        out_ref, bias_ref, class_ref, turned_ref = refs
    else:
        acc_out, stat_out, bias_ref, class_ref, turned_ref = refs
    tokens = q_ref.shape[0]
    sizes = [key_ref.shape[0] for key_ref, _ in sources]

    @pl.when(pl.program_id(0) == 0)
    def _():
        position = lax.axis_index("frame")
        row = lax.broadcasted_iota(jnp.int32, (tokens, HD), 0) // COLS
        lane = lax.broadcasted_iota(jnp.int32, (tokens, HD), 1)
        bias = jnp.zeros((tokens, HD), jnp.float32)
        base, start = 0, 0
        for (windowed, there), size in zip(kinds, sizes):
            there = there(position)
            if windowed:
                wide = size // COLS
                here = jnp.abs(row - (lane - base)) <= jnp.where(there, window_ref[0], -1)
                hot = row[:size] == lane[:size] - base
            else:
                wide = 1
                here = lane * 0 + jnp.where(there, 1, 0) > 0
                hot = lane[:size] == base
            mine = (lane >= base) & (lane < base + wide)
            bias = jnp.where(mine & ~here, MASKED, bias)
            class_ref[pl.ds(start, size), :] = jnp.where(hot, 1.0, 0.0).astype(jnp.bfloat16)
            base, start = base + wide, start + size
        bias_ref[...] = bias.astype(jnp.bfloat16)
        turned_ref[:, pl.ds(HD, ONES), :] = jnp.ones((together, ONES, sum(sizes)), jnp.bfloat16)

    def column(head):
        return pl.ds(head * HD, HD)

    def scores_of(head):
        keys = jnp.concatenate([key_ref[:, column(head)] for key_ref, _ in sources], axis=0)
        keys = jnp.concatenate([keys, class_ref[...]], axis=1)
        query = jnp.concatenate([q_ref[:, column(head)], bias_ref[...]], axis=1)
        scores = lax.dot_general(
            keys, query, (((1,), (1,)), ((), ())), preferred_element_type=jnp.float32
        )
        return scores, jnp.max(scores, axis=0, keepdims=True)

    for head in range(together):
        start = 0
        for (_, value_ref), size in zip(sources, sizes):
            turned_ref[head, pl.ds(0, HD), pl.ds(start, size)] = value_ref[:, column(head)].T
            start += size
    upcoming = scores_of(0)
    for head in range(together):
        scores, peak = upcoming
        if head + 1 < together:
            upcoming = scores_of(head + 1)
        if not first:
            before = stat_in[8 * head : 8 * head + 1, :]
            peak = jnp.maximum(peak, before)
        weights = jnp.exp2((scores - peak) * BASE2).astype(jnp.bfloat16)
        total = jnp.dot(turned_ref[head], weights, preferred_element_type=jnp.float32)
        acc, norm = total[:HD, :], total[HD : HD + 1, :]
        if not first:
            scale = jnp.exp2((before - peak) * BASE2)
            acc = acc + acc_in[column(head), :] * scale
            norm = norm + stat_in[8 * head + 1 : 8 * head + 2, :] * scale
        if last:
            out_ref[:, column(head)] = (acc / norm).T.astype(out_ref.dtype)
        else:
            acc_out[column(head), :] = acc
            stat_out[8 * head : 8 * head + 1, :] = peak
            stat_out[8 * head + 1 : 8 * head + 2, :] = norm


def attend(window, query, sources, state, last):
    tokens, width = query.shape
    heads = width // HD
    together = next(n for n in (3, 2, 1) if heads % n == 0)
    kinds = tuple(source[4:] for source in sources)

    def columns(rows, base):
        return pl.BlockSpec((rows, HD * together), lambda h, window: (0, base // together + h))

    specs, operands = [columns(tokens, 0)], [query]
    keys_count = 0
    for key, key_base, value, value_base, _, _ in sources:
        specs += [columns(key.shape[0], key_base), columns(key.shape[0], value_base)]
        operands += [key, value]
        keys_count += key.shape[0]
    state_specs = [
        pl.BlockSpec((HD * together, tokens), lambda h, window: (h, 0)),
        pl.BlockSpec((8 * together, tokens), lambda h, window: (h, 0)),
    ]
    moved_bytes = 2 * (tokens + 2 * keys_count) * width
    if state is not None:
        specs += state_specs
        operands += list(state)
        moved_bytes += 4 * tokens * width
    if last:
        out_shape = jax.ShapeDtypeStruct((tokens, width), jnp.bfloat16)
        out_specs = columns(tokens, 0)
    else:
        out_shape = [
            jax.ShapeDtypeStruct((width, tokens), jnp.float32),
            jax.ShapeDtypeStruct((8 * heads, tokens), jnp.float32),
        ]
        out_specs = state_specs
    return pl.pallas_call(
        functools.partial(attend_kernel, kinds, together, state is None, last),
        out_shape=out_shape,
        grid_spec=pltpu.PrefetchScalarGridSpec(
            num_scalar_prefetch=1,
            grid=(heads // together,),
            in_specs=specs,
            out_specs=out_specs,
            scratch_shapes=[
                pltpu.VMEM((tokens, HD), jnp.bfloat16),
                pltpu.VMEM((keys_count, HD), jnp.bfloat16),
                pltpu.VMEM((together, HD + ONES, keys_count), jnp.bfloat16),
            ],
        ),
        compiler_params=pltpu.CompilerParams(vmem_limit_bytes=67_043_328),
        cost_estimate=pl.CostEstimate(
            flops=4 * tokens * keys_count * width,
            bytes_accessed=moved_bytes + 2 * tokens * width,
            transcendentals=tokens * keys_count * heads,
        ),
    )(window, *operands)


def body(query_in, keys_in, values_in, far_picks, win_rows):
    frames = lax.axis_size("frame")
    query, keys, values = query_in[0], keys_in[0], values_in[0]
    heads = query.shape[1] // HD
    offsets = offsets_for(frames)
    shared = frames % 2 == 0 and 2 in offsets

    def beyond_of(position):
        return position + 2 * (position % 2) - 1

    def there(frame):
        return (frame >= 0) & (frame < frames)

    outward = [(1, is_odd), (-1, is_even)]
    inward = [(1, is_even), (-1, is_odd)]
    beyond_keys = moved(keys, outward)
    beyond_values = moved(values, outward)
    beyond = [beyond_keys, beyond_values]

    far = []
    for column in sorted(range(len(offsets)), key=lambda c: -abs(offsets[c])):
        offset = offsets[column]
        if shared and abs(offset) == 2:
            continue
        if 2 * abs(offset) == frames:
            if offset > 0:
                continue
            back, ahead = column, offsets.index(-offset)
            half = -offset

            def across(position, half=half, back=back, ahead=ahead):
                low = position < half
                return position + jnp.where(low, half, -half), jnp.where(low, back, ahead)

            steps = [(half, lambda f, half=half: f < half), (-half, lambda f, half=half: f >= half)]
            far.append((steps, across, lambda position: position >= 0))
            continue
        far.append(
            (
                [(-offset, anyone)],
                lambda position, offset=offset, column=column: (position - offset, column),
                lambda position, offset=offset: there(position + offset),
            )
        )
    if shared:
        back, ahead = offsets.index(-2), offsets.index(2)

        def two_on(position):
            odd = position % 2
            return position + 2 - 4 * odd, jnp.where(odd == 0, back, ahead)

        def two_back(position):
            return there(position - 2 + 4 * (position % 2))

        def partner(position):
            odd = position % 2
            return position + 1 - 2 * odd, jnp.where(odd == 0, back, ahead)

        far.append(([(2, is_even), (-2, is_odd)], two_on, two_back))
    blocks = gather(far_picks, keys, values, [reader for _, reader, _ in far], frames)
    arrived = []
    for block, (steps, _, _) in zip(blocks, far):
        arrived.append(moved(block, steps))
    mate_keys = moved(keys, inward)
    mate_values = moved(values, inward)

    def always(position):
        return position >= 0

    def near_there(position):
        return there(beyond_of(position))

    own = [(keys, 0, values, 0, True, always), (mate_keys, 0, mate_values, 0, True, always)]
    state = attend(win_rows, query, own, None, False)
    nearby = [(beyond[0], 0, beyond[1], 0, True, near_there)]
    if shared:
        (handed,) = gather(far_picks, *beyond, [partner], frames)
        handed = moved(handed, inward)
        nearby.append(
            (handed, 0, handed, heads, False, lambda p: there(p + 2 - 4 * (p % 2)))
        )
    state = attend(win_rows, query, nearby, state, False)
    distant = [
        (block, 0, block, heads, False, there) for block, (_, _, there) in zip(arrived, far)
    ]
    return attend(win_rows, query, distant, state, True)[None]


def solution(mesh):
    in_specs = (
        P(("groups", "frame"), None, None),
        P(("groups", "frame"), None, None),
        P(("groups", "frame"), None, None),
        P("groups", None),
        P(("groups", "frame")),
    )
    out_specs = P(("groups", "frame"), None, None)

    return jax.shard_map(body, mesh=mesh, in_specs=in_specs, out_specs=out_specs, check_vma=False)
```

```python
import functools
import math

import jax
import jax.numpy as jnp
from jax import lax
from jax.experimental import pallas as pl
from jax.experimental.pallas import tpu as pltpu
from jax.sharding import PartitionSpec as P

HD = 128
COLS = 32
SUB = 128
NREACH = 3
MASKED = -1e30
BASE2 = math.log2(math.e) / math.sqrt(HD)
ONES = 16


def offsets_for(frames):
    spacing = [frames // 2 ** (NREACH - level_index) for level_index in range(NREACH)]
    return [-stride for stride in spacing] + [stride for stride in spacing]


def moved(value, steps):
    count = lax.axis_size("frame")
    pairs = [(f, f + step) for step, who in steps for f in range(count) if who(f)]
    pairs = [(source, target) for source, target in pairs if 0 <= target < count]
    return lax.ppermute(value, "frame", pairs)


def anyone(frame):
    return True


def is_even(frame):
    return frame % 2 == 0


def is_odd(frame):
    return frame % 2 == 1


def gather_kernel(readers, frames, picks_ref, keys_ref, values_ref, *refs):
    outs, sems = refs[: len(readers)], refs[len(readers)]
    width = keys_ref.shape[1]
    position = lax.axis_index("frame")
    copies = []
    for slot, (reader_of, out) in enumerate(zip(readers, outs)):
        reader, column = reader_of(position)
        pick = picks_ref[column, jnp.clip(reader, 0, frames - 1)]
        rows = pl.ds(pl.multiple_of(pick * SUB, SUB), SUB)
        for half, source in enumerate((keys_ref, values_ref)):
            target = out.at[:, pl.ds(half * width, width)]
            copies.append(
                pltpu.make_async_copy(source.at[rows, :], target, sems.at[2 * slot + half])
            )
    for copy in copies:
        copy.start()
    for copy in copies:
        copy.wait()


def gather(picks, keys, values, readers, frames):
    width = keys.shape[1]
    shape = (SUB, 2 * width)
    return pl.pallas_call(
        functools.partial(gather_kernel, readers, frames),
        out_shape=[jax.ShapeDtypeStruct(shape, keys.dtype) for _ in readers],
        in_specs=[
            pl.BlockSpec(memory_space=pltpu.SMEM),
            pl.BlockSpec(memory_space=pltpu.HBM),
            pl.BlockSpec(memory_space=pltpu.HBM),
        ],
        out_specs=[pl.BlockSpec(memory_space=pltpu.VMEM) for _ in readers],
        scratch_shapes=[pltpu.SemaphoreType.DMA((2 * len(readers),))],
        compiler_params=pltpu.CompilerParams(vmem_limit_bytes=67_043_328),
        cost_estimate=pl.CostEstimate(
            flops=0, bytes_accessed=8 * SUB * width * len(readers), transcendentals=0
        ),
    )(picks.T, keys, values)


def attend_kernel(kinds, together, first, last, onto, window_ref, q_ref, *refs):
    count = len(kinds)
    sources = [(refs[2 * i], refs[2 * i + 1]) for i in range(count)]
    refs = refs[2 * count :]
    if not first:
        acc_in, stat_in = refs[:2]
        refs = refs[2:]
    if onto:
        refs = refs[1:]
    if last:
        out_ref, bias_ref, class_ref, turned_ref = refs
    else:
        acc_out, stat_out, bias_ref, class_ref, turned_ref = refs
    tokens = q_ref.shape[0]
    sizes = [key_ref.shape[0] for key_ref, _ in sources]

    @pl.when(pl.program_id(0) == 0)
    def _():
        position = lax.axis_index("frame")
        row = lax.broadcasted_iota(jnp.int32, (tokens, HD), 0) // COLS
        lane = lax.broadcasted_iota(jnp.int32, (tokens, HD), 1)
        bias = jnp.zeros((tokens, HD), jnp.float32)
        base, start = 0, 0
        for (windowed, there), size in zip(kinds, sizes):
            there = there(position)
            if windowed:
                wide = size // COLS
                here = jnp.abs(row - (lane - base)) <= jnp.where(there, window_ref[0], -1)
                hot = row[:size] == lane[:size] - base
            else:
                wide = 1
                here = lane * 0 + jnp.where(there, 1, 0) > 0
                hot = lane[:size] == base
            mine = (lane >= base) & (lane < base + wide)
            bias = jnp.where(mine & ~here, MASKED, bias)
            class_ref[pl.ds(start, size), :] = jnp.where(hot, 1.0, 0.0).astype(jnp.bfloat16)
            base, start = base + wide, start + size
        bias_ref[...] = bias.astype(jnp.bfloat16)
        turned_ref[:, pl.ds(HD, ONES), :] = jnp.ones((together, ONES, sum(sizes)), jnp.bfloat16)

    def column(head):
        return pl.ds(head * HD, HD)

    def scores_of(head):
        keys = jnp.concatenate([key_ref[:, column(head)] for key_ref, _ in sources], axis=0)
        keys = jnp.concatenate([keys, class_ref[...]], axis=1)
        query = jnp.concatenate([q_ref[:, column(head)], bias_ref[...]], axis=1)
        scores = lax.dot_general(
            keys, query, (((1,), (1,)), ((), ())), preferred_element_type=jnp.float32
        )
        return scores, jnp.max(scores, axis=0, keepdims=True)

    for head in range(together):
        start = 0
        for (_, value_ref), size in zip(sources, sizes):
            turned_ref[head, pl.ds(0, HD), pl.ds(start, size)] = value_ref[:, column(head)].T
            start += size
    upcoming = scores_of(0)
    for head in range(together):
        scores, peak = upcoming
        if head + 1 < together:
            upcoming = scores_of(head + 1)
        if not first:
            before = stat_in[8 * head : 8 * head + 1, :]
            peak = jnp.maximum(peak, before)
        weights = jnp.exp2((scores - peak) * BASE2).astype(jnp.bfloat16)
        total = jnp.dot(turned_ref[head], weights, preferred_element_type=jnp.float32)
        acc, norm = total[:HD, :], total[HD : HD + 1, :]
        if not first:
            scale = jnp.exp2((before - peak) * BASE2)
            acc = acc + acc_in[column(head), :] * scale
            norm = norm + stat_in[8 * head + 1 : 8 * head + 2, :] * scale
        if last:
            out_ref[:, column(head)] = (acc / norm).T.astype(out_ref.dtype)
        else:
            acc_out[column(head), :] = acc
            stat_out[8 * head : 8 * head + 1, :] = peak
            stat_out[8 * head + 1 : 8 * head + 2, :] = norm


def attend(window, query, sources, part, state, last, target=None):
    tokens, width = query.shape
    first_head, heads = part
    together = next(n for n in (3, 2, 1) if heads % n == 0 and first_head % n == 0)
    kinds = tuple(source[4:] for source in sources)

    def columns(rows, base):
        return pl.BlockSpec((rows, HD * together), lambda h, window: (0, base // together + h))

    def state_specs(base):
        return [
            pl.BlockSpec((HD * together, tokens), lambda h, window: (base // together + h, 0)),
            pl.BlockSpec((8 * together, tokens), lambda h, window: (base // together + h, 0)),
        ]

    specs, operands = [columns(tokens, first_head)], [query]
    keys_count = 0
    for key, key_base, value, value_base, _, _ in sources:
        specs += [columns(key.shape[0], key_base), columns(key.shape[0], value_base)]
        operands += [key, value]
        keys_count += key.shape[0]
    moved_bytes = 2 * (tokens + 2 * keys_count) * heads * HD
    if state is not None:
        specs += state_specs(state[2])
        operands += state[:2]
        moved_bytes += 4 * tokens * heads * HD
    aliases = {}
    if last:
        out_shape = jax.ShapeDtypeStruct((tokens, width), jnp.bfloat16)
        out_specs = columns(tokens, first_head)
        if target is not None:
            aliases = {1 + len(operands): 0}
            specs.append(pl.BlockSpec(memory_space=pl.ANY))
            operands.append(target)
    else:
        out_shape = [
            jax.ShapeDtypeStruct((HD * heads, tokens), jnp.float32),
            jax.ShapeDtypeStruct((8 * heads, tokens), jnp.float32),
        ]
        out_specs = state_specs(0)
    return pl.pallas_call(
        functools.partial(
            attend_kernel, kinds, together, state is None, last, target is not None
        ),
        out_shape=out_shape,
        grid_spec=pltpu.PrefetchScalarGridSpec(
            num_scalar_prefetch=1,
            grid=(heads // together,),
            in_specs=specs,
            out_specs=out_specs,
            scratch_shapes=[
                pltpu.VMEM((tokens, HD), jnp.bfloat16),
                pltpu.VMEM((keys_count, HD), jnp.bfloat16),
                pltpu.VMEM((together, HD + ONES, keys_count), jnp.bfloat16),
            ],
        ),
        input_output_aliases=aliases,
        compiler_params=pltpu.CompilerParams(vmem_limit_bytes=67_043_328),
        cost_estimate=pl.CostEstimate(
            flops=4 * tokens * keys_count * heads * HD,
            bytes_accessed=moved_bytes + 2 * tokens * heads * HD,
            transcendentals=tokens * keys_count * heads,
        ),
    )(window, *operands)


def body(query_in, keys_in, values_in, far_picks, win_rows):
    frames = lax.axis_size("frame")
    query, keys, values = query_in[0], keys_in[0], values_in[0]
    heads = query.shape[1] // HD
    offsets = offsets_for(frames)
    shared = frames % 2 == 0 and 2 in offsets

    def beyond_of(position):
        return position + 2 * (position % 2) - 1

    def there(frame):
        return (frame >= 0) & (frame < frames)

    outward = [(1, is_odd), (-1, is_even)]
    inward = [(1, is_even), (-1, is_odd)]
    half_heads = heads // 2
    halves = [(0, half_heads), (half_heads, heads - half_heads)]
    beyond = []
    for half, (start, count) in enumerate(halves):
        part = slice(start * HD, (start + count) * HD)
        beyond_keys = moved(keys[:, part], outward)
        beyond_values = moved(values[:, part], outward)
        beyond.append((beyond_keys, beyond_values))

    far = []
    for column in sorted(range(len(offsets)), key=lambda c: -abs(offsets[c])):
        offset = offsets[column]
        if shared and abs(offset) == 2:
            continue
        if 2 * abs(offset) == frames:
            if offset > 0:
                continue
            back, ahead = column, offsets.index(-offset)
            half = -offset

            def across(position, half=half, back=back, ahead=ahead):
                low = position < half
                return position + jnp.where(low, half, -half), jnp.where(low, back, ahead)

            steps = [(half, lambda f, half=half: f < half), (-half, lambda f, half=half: f >= half)]
            far.append((steps, across, lambda position: position >= 0))
            continue
        far.append(
            (
                [(-offset, anyone)],
                lambda position, offset=offset, column=column: (position - offset, column),
                lambda position, offset=offset: there(position + offset),
            )
        )
    if shared:
        back, ahead = offsets.index(-2), offsets.index(2)

        def two_on(position):
            odd = position % 2
            return position + 2 - 4 * odd, jnp.where(odd == 0, back, ahead)

        def two_back(position):
            return there(position - 2 + 4 * (position % 2))

        def partner(position):
            odd = position % 2
            return position + 1 - 2 * odd, jnp.where(odd == 0, back, ahead)

        far.append(([(2, is_even), (-2, is_odd)], two_on, two_back))
    blocks = gather(far_picks, keys, values, [reader for _, reader, _ in far], frames)
    arrived = []
    for block, (steps, _, _) in zip(blocks, far):
        arrived.append(moved(block, steps))
    mate_keys = moved(keys, inward)
    mate_values = moved(values, inward)

    def always(position):
        return position >= 0

    def near_there(position):
        return there(beyond_of(position))

    def ahead_there(position):
        return there(position + 2 - 4 * (position % 2))

    own = [(keys, 0, values, 0, True, always), (mate_keys, 0, mate_values, 0, True, always)]
    state = attend(win_rows, query, own, (0, heads), None, False)

    def nearby(half, state, last, target):
        keys, values = beyond[half]
        sources = [(keys, 0, values, 0, True, near_there)]
        if shared:
            (block,) = gather(far_picks, keys, values, [partner], frames)
            block = moved(block, inward)
            sources.append((block, 0, block, halves[half][1], False, ahead_there))
        return attend(win_rows, query, sources, halves[half], state, last, target)

    def distant(half, state, last):
        start = halves[half][0]
        sources = [
            (block, start, block, heads + start, False, there)
            for block, (_, _, there) in zip(arrived, far)
        ]
        return attend(win_rows, query, sources, halves[half], state, last)

    low = nearby(0, (*state, 0), False, None)
    high = distant(1, (*state, half_heads), False)
    out = distant(0, (*low, 0), True)
    return nearby(1, (*high, 0), True, out)[None]


def solution(mesh):
    in_specs = (
        P(("groups", "frame"), None, None),
        P(("groups", "frame"), None, None),
        P(("groups", "frame"), None, None),
        P("groups", None),
        P(("groups", "frame")),
    )
    out_specs = P(("groups", "frame"), None, None)

    return jax.shard_map(body, mesh=mesh, in_specs=in_specs, out_specs=out_specs, check_vma=False)
```

```python
import functools
import math

import jax
import jax.numpy as jnp
from jax import lax
from jax.experimental import pallas as pl
from jax.experimental.pallas import tpu as pltpu
from jax.sharding import PartitionSpec as P

HD = 128
COLS = 32
SUB = 128
NREACH = 3
MASKED = -1e30
BASE2 = math.log2(math.e) / math.sqrt(HD)
ONES = 16


def offsets_for(frames):
    spacing = [frames // 2 ** (NREACH - level_index) for level_index in range(NREACH)]
    return [-stride for stride in spacing] + [stride for stride in spacing]


def moved(value, steps):
    count = lax.axis_size("frame")
    pairs = [(f, f + step) for step, who in steps for f in range(count) if who(f)]
    pairs = [(source, target) for source, target in pairs if 0 <= target < count]
    return lax.ppermute(value, "frame", pairs)


def anyone(frame):
    return True


def is_even(frame):
    return frame % 2 == 0


def is_odd(frame):
    return frame % 2 == 1


def gather_kernel(readers, frames, count, instead, picks_ref, *refs):
    arrays, outs = refs[:count], refs[count : count + len(readers)]
    sems = refs[count + len(readers)]
    position = lax.axis_index("frame")

    def copy_all(arrays):
        copies = []
        for slot, (reader_of, out) in enumerate(zip(readers, outs)):
            reader, column = reader_of(position)
            pick = picks_ref[column, jnp.clip(reader, 0, frames - 1)]
            rows = pl.ds(pl.multiple_of(pick * SUB, SUB), SUB)
            start = 0
            for which, source in enumerate(arrays):
                target = out.at[:, pl.ds(start, source.shape[1])]
                sem = sems.at[count * slot + which]
                copies.append(pltpu.make_async_copy(source.at[rows, :], target, sem))
                start += source.shape[1]
        for copy in copies:
            copy.start()
        for copy in copies:
            copy.wait()

    if instead is None:
        copy_all(arrays)
    else:
        pl.when(instead(position))(lambda: copy_all([*arrays[:-2], arrays[-1]]))
        pl.when(jnp.logical_not(instead(position)))(lambda: copy_all(arrays[:-1]))


def gather(picks, arrays, readers, frames, instead=None):
    width = sum(array.shape[1] for array in (arrays if instead is None else arrays[:-1]))
    return pl.pallas_call(
        functools.partial(gather_kernel, readers, frames, len(arrays), instead),
        out_shape=[jax.ShapeDtypeStruct((SUB, width), arrays[0].dtype) for _ in readers],
        in_specs=[
            pl.BlockSpec(memory_space=pltpu.SMEM),
            *[pl.BlockSpec(memory_space=pltpu.HBM)] * len(arrays),
        ],
        out_specs=[pl.BlockSpec(memory_space=pltpu.VMEM) for _ in readers],
        scratch_shapes=[pltpu.SemaphoreType.DMA((len(arrays) * len(readers),))],
        compiler_params=pltpu.CompilerParams(vmem_limit_bytes=67_043_328),
        cost_estimate=pl.CostEstimate(
            flops=0, bytes_accessed=4 * SUB * width * len(readers), transcendentals=0
        ),
    )(picks.T, *arrays)


def attend_kernel(kinds, together, first, last, window_ref, q_ref, *refs):
    sources = []
    for _, _, instead in kinds:
        count = 2 if instead is None else 3
        sources.append(refs[:count])
        refs = refs[count:]
    if not first:
        acc_in, stat_in = refs[:2]
        refs = refs[2:]
    if last:
        out_ref, bias_ref, class_ref, turned_ref = refs
    else:
        acc_out, stat_out, bias_ref, class_ref, turned_ref = refs
    tokens = q_ref.shape[0]
    sizes = [source[0].shape[0] for source in sources]
    position = lax.axis_index("frame")

    @pl.when(pl.program_id(0) == 0)
    def _():
        row = lax.broadcasted_iota(jnp.int32, (tokens, HD), 0) // COLS
        lane = lax.broadcasted_iota(jnp.int32, (tokens, HD), 1)
        bias = jnp.zeros((tokens, HD), jnp.float32)
        base, start = 0, 0
        for (windowed, there, _), size in zip(kinds, sizes):
            there = there(position)
            if windowed:
                wide = size // COLS
                here = jnp.abs(row - (lane - base)) <= jnp.where(there, window_ref[0], -1)
                hot = row[:size] == lane[:size] - base
            else:
                wide = 1
                here = lane * 0 + jnp.where(there, 1, 0) > 0
                hot = lane[:size] == base
            mine = (lane >= base) & (lane < base + wide)
            bias = jnp.where(mine & ~here, MASKED, bias)
            class_ref[pl.ds(start, size), :] = jnp.where(hot, 1.0, 0.0).astype(jnp.bfloat16)
            base, start = base + wide, start + size
        bias_ref[...] = bias.astype(jnp.bfloat16)
        turned_ref[:, pl.ds(HD, ONES), :] = jnp.ones((together, ONES, sum(sizes)), jnp.bfloat16)

    def column(head):
        return pl.ds(head * HD, HD)

    def scores_of(head):
        keys = jnp.concatenate([source[0][:, column(head)] for source in sources], axis=0)
        keys = jnp.concatenate([keys, class_ref[...]], axis=1)
        query = jnp.concatenate([q_ref[:, column(head)], bias_ref[...]], axis=1)
        scores = lax.dot_general(
            keys, query, (((1,), (1,)), ((), ())), preferred_element_type=jnp.float32
        )
        return scores, jnp.max(scores, axis=0, keepdims=True)

    for head in range(together):
        start = 0
        for source, (_, _, instead), size in zip(sources, kinds, sizes):
            value = source[1][:, column(head)]
            if instead is not None:
                value = jnp.where(instead(position), source[2][:, column(head)], value)
            turned_ref[head, pl.ds(0, HD), pl.ds(start, size)] = value.T
            start += size
    upcoming = scores_of(0)
    for head in range(together):
        scores, peak = upcoming
        if head + 1 < together:
            upcoming = scores_of(head + 1)
        if not first:
            before = stat_in[8 * head : 8 * head + 1, :]
            peak = jnp.maximum(peak, before)
        weights = jnp.exp2((scores - peak) * BASE2).astype(jnp.bfloat16)
        total = jnp.dot(turned_ref[head], weights, preferred_element_type=jnp.float32)
        acc, norm = total[:HD, :], total[HD : HD + 1, :]
        if not first:
            scale = jnp.exp2((before - peak) * BASE2)
            acc = acc + acc_in[column(head), :] * scale
            norm = norm + stat_in[8 * head + 1 : 8 * head + 2, :] * scale
        if last:
            out_ref[:, column(head)] = (acc / norm).T.astype(out_ref.dtype)
        else:
            acc_out[column(head), :] = acc
            stat_out[8 * head : 8 * head + 1, :] = peak
            stat_out[8 * head + 1 : 8 * head + 2, :] = norm


def attend(window, query, sources, state, last, part=None):
    tokens, width = query.shape
    first_head, heads = part or (0, width // HD)
    together = next(n for n in (3, 2, 1) if heads % n == 0 and first_head % n == 0)
    kinds = tuple((*source[4:6], source[7] if source[6:] else None) for source in sources)

    def columns(rows, base):
        return pl.BlockSpec((rows, HD * together), lambda h, window: (0, base // together + h))

    specs, operands = [columns(tokens, first_head)], [query]
    keys_count = 0
    for key, key_base, value, value_base, _, _, *other in sources:
        specs += [columns(key.shape[0], key_base), columns(key.shape[0], value_base)]
        operands += [key, value]
        if other:
            specs.append(columns(key.shape[0], value_base))
            operands.append(other[0])
        keys_count += key.shape[0]
    base = first_head // together
    state_specs = [
        pl.BlockSpec((HD * together, tokens), lambda h, window: (base + h, 0)),
        pl.BlockSpec((8 * together, tokens), lambda h, window: (base + h, 0)),
    ]
    moved_bytes = 2 * (tokens + 2 * keys_count) * heads * HD
    aliases = {}
    if state is not None:
        if not last:
            aliases = {1 + len(operands): 0, 2 + len(operands): 1}
        specs += state_specs
        operands += list(state)
        moved_bytes += 4 * tokens * heads * HD
    if last:
        out_shape = jax.ShapeDtypeStruct((tokens, width), jnp.bfloat16)
        out_specs = columns(tokens, first_head)
    else:
        out_shape = [
            jax.ShapeDtypeStruct((width, tokens), jnp.float32),
            jax.ShapeDtypeStruct((width // HD * 8, tokens), jnp.float32),
        ]
        out_specs = state_specs
    return pl.pallas_call(
        functools.partial(attend_kernel, kinds, together, state is None, last),
        out_shape=out_shape,
        grid_spec=pltpu.PrefetchScalarGridSpec(
            num_scalar_prefetch=1,
            grid=(heads // together,),
            in_specs=specs,
            out_specs=out_specs,
            scratch_shapes=[
                pltpu.VMEM((tokens, HD), jnp.bfloat16),
                pltpu.VMEM((keys_count, HD), jnp.bfloat16),
                pltpu.VMEM((together, HD + ONES, keys_count), jnp.bfloat16),
            ],
        ),
        input_output_aliases=aliases,
        compiler_params=pltpu.CompilerParams(vmem_limit_bytes=67_043_328),
        cost_estimate=pl.CostEstimate(
            flops=4 * tokens * keys_count * heads * HD,
            bytes_accessed=moved_bytes + 2 * tokens * heads * HD,
            transcendentals=tokens * keys_count * heads,
        ),
    )(window, *operands)


def body(query_in, keys_in, values_in, far_picks, win_rows):
    frames = lax.axis_size("frame")
    query, keys, values = query_in[0], keys_in[0], values_in[0]
    heads = query.shape[1] // HD
    offsets = offsets_for(frames)
    shared = frames % 2 == 0 and 2 in offsets

    def beyond_of(position):
        return position + 2 * (position % 2) - 1

    def there(frame):
        return (frame >= 0) & (frame < frames)

    outward = [(1, is_odd), (-1, is_even)]
    inward = [(1, is_even), (-1, is_odd)]
    hop = [(-2, lambda f: f % 4 == 3 and f + 1 < frames), (2, lambda f: f % 4 == 0 and f > 0)]
    skip = [(3, lambda f: f % 4 == 1), (-3, lambda f: f % 4 == 2)]

    def turning(position):
        return (position + 1) % 4 < 2

    beyond_keys = moved(keys, outward)
    half = heads // 2
    halves = [(0, half), (half, heads - half)]
    beyond_values = []
    for which, (start, number) in enumerate(halves):
        columns = values[:, start * HD : (start + number) * HD]
        steps = outward
        if shared and which == 1:
            around = moved(columns, hop)
            steps = [(1, lambda f: f % 4 == 1), (-1, lambda f: f % 4 == 2)]
        beyond_values.append(moved(columns, steps))

    far = []
    for column in sorted(range(len(offsets)), key=lambda c: -abs(offsets[c])):
        offset = offsets[column]
        if shared and abs(offset) == 2:
            continue
        if 2 * abs(offset) == frames:
            if offset > 0:
                continue
            back, ahead = column, offsets.index(-offset)
            half = -offset

            def across(position, half=half, back=back, ahead=ahead):
                low = position < half
                return position + jnp.where(low, half, -half), jnp.where(low, back, ahead)

            steps = [(half, lambda f, half=half: f < half), (-half, lambda f, half=half: f >= half)]
            far.append((steps, across, lambda position: position >= 0))
            continue
        far.append(
            (
                [(-offset, anyone)],
                lambda position, offset=offset, column=column: (position - offset, column),
                lambda position, offset=offset: there(position + offset),
            )
        )
    if shared:
        back, ahead = offsets.index(-2), offsets.index(2)

        def past(position):
            odd = position % 2
            return position - 1 + 2 * odd, jnp.where(odd == 0, ahead, back)

        def two_back(position):
            return there(position - 2 + 4 * (position % 2))

        def partner(position):
            odd = position % 2
            return position + 1 - 2 * odd, jnp.where(odd == 0, back, ahead)

    blocks = gather(far_picks, [keys, values], [reader for _, reader, _ in far], frames)
    arrived = []
    for block, (steps, _, _) in zip(blocks, far):
        arrived.append(moved(block, steps))
    mate_keys = moved(keys, inward)
    mate_values = moved(values, inward)

    if shared:
        (behind,) = gather(far_picks, [mate_keys, mate_values], [past], frames)
        behind = moved(behind, outward)
        around = moved(around, skip)

    def always(position):
        return position >= 0

    def near_there(position):
        return there(beyond_of(position))

    def ahead_there(position):
        return there(position + 2 - 4 * (position % 2))

    own = [(keys, 0, values, 0, True, always), (mate_keys, 0, mate_values, 0, True, always)]
    state = attend(win_rows, query, own, None, False)
    distant = [
        (block, 0, block, heads, False, there) for block, (_, _, there) in zip(arrived, far)
    ]
    if shared:
        state = attend(win_rows, query, distant, state, False)
    for which, part in enumerate(halves):
        nearby = [(beyond_keys, part[0], beyond_values[which], 0, True, near_there)]
        if shared and which == 1:
            nearby = [(*nearby[0], around, turning)]
        state = attend(win_rows, query, nearby, state, False, part)
    if not shared:
        return attend(win_rows, query, distant, state, True)[None]
    whole = [beyond_keys, *beyond_values, around]
    (handed,) = gather(far_picks, whole, [partner], frames, turning)
    handed = moved(handed, inward)
    rest = [
        (handed, 0, handed, heads, False, ahead_there),
        (behind, 0, behind, heads, False, two_back),
    ]
    return attend(win_rows, query, rest, state, True)[None]


def solution(mesh):
    in_specs = (
        P(("groups", "frame"), None, None),
        P(("groups", "frame"), None, None),
        P(("groups", "frame"), None, None),
        P("groups", None),
        P(("groups", "frame")),
    )
    out_specs = P(("groups", "frame"), None, None)

    return jax.shard_map(body, mesh=mesh, in_specs=in_specs, out_specs=out_specs, check_vma=False)
```

```python
import functools
import math

import jax
import jax.numpy as jnp
from jax import lax
from jax.experimental import pallas as pl
from jax.experimental.pallas import tpu as pltpu
from jax.sharding import PartitionSpec as P

HD = 128
COLS = 32
SUB = 128
NREACH = 3
MASKED = -1e30
BASE2 = math.log2(math.e) / math.sqrt(HD)
ONES = 16


def offsets_for(frames):
    spacing = [frames // 2 ** (NREACH - level_index) for level_index in range(NREACH)]
    return [-stride for stride in spacing] + [stride for stride in spacing]


def moved(value, steps):
    count = lax.axis_size("frame")
    pairs = [(f, f + step) for step, who in steps for f in range(count) if who(f)]
    pairs = [(source, target) for source, target in pairs if 0 <= target < count]
    return lax.ppermute(value, "frame", pairs)


def anyone(frame):
    return True


def is_even(frame):
    return frame % 2 == 0


def is_odd(frame):
    return frame % 2 == 1


def gather_kernel(readers, frames, count, parts, picks_ref, *refs):
    arrays, outs = refs[:count], refs[count:-1]
    sems = refs[-1]
    position = lax.axis_index("frame")
    copies = []

    def copy(source, target):
        copies.append(pltpu.make_async_copy(source, target, sems.at[len(copies)]))

    def block(pick):
        return pl.ds(pl.multiple_of(pick * SUB, SUB), SUB)

    def pick_of(reader_of):
        reader, column = reader_of(position)
        return picks_ref[column, jnp.clip(reader, 0, frames - 1)]

    for reader_of, out in zip(readers[:-1] if parts else readers, outs):
        rows = block(pick_of(reader_of))
        start = 0
        for source in arrays:
            copy(source.at[rows, :], out.at[:, pl.ds(start, source.shape[1])])
            start += source.shape[1]
    if parts:
        pick, source = pick_of(readers[-1]), arrays[-1]
        outs = outs[len(readers) - 1 :]
        copy(source.at[block(pick), :], outs[0])
        for (start, width), out in zip(parts, outs[1:]):
            for other in range(source.shape[0] // SUB - 1):
                rows = block(other + jnp.where(other >= pick, 1, 0))
                target = out.at[pl.ds(other * SUB, SUB), :]
                copy(source.at[rows, pl.ds(start, width)], target)
    for each in copies:
        each.start()
    for each in copies:
        each.wait()


def gather(picks, arrays, readers, frames, parts=()):
    width = sum(array.shape[1] for array in arrays)
    dtype = arrays[0].dtype
    shapes = [(SUB, width)] * (len(readers) - bool(parts))
    count = len(shapes) * len(arrays)
    if parts:
        tokens, last_width = arrays[-1].shape
        shapes += [(SUB, last_width)] + [(tokens - SUB, width) for _, width in parts]
        count += 1 + (tokens // SUB - 1) * len(parts)
    return pl.pallas_call(
        functools.partial(gather_kernel, readers, frames, len(arrays), parts),
        out_shape=[jax.ShapeDtypeStruct(shape, dtype) for shape in shapes],
        in_specs=[
            pl.BlockSpec(memory_space=pltpu.SMEM),
            *[pl.BlockSpec(memory_space=pltpu.HBM)] * len(arrays),
        ],
        out_specs=[pl.BlockSpec(memory_space=pltpu.VMEM) for _ in shapes],
        scratch_shapes=[pltpu.SemaphoreType.DMA((count,))],
        compiler_params=pltpu.CompilerParams(vmem_limit_bytes=67_043_328),
        cost_estimate=pl.CostEstimate(
            flops=0,
            bytes_accessed=4 * sum(rows * columns for rows, columns in shapes),
            transcendentals=0,
        ),
    )(picks.T, *arrays)


def attend_kernel(kinds, together, first, last, onto, window_ref, picks_ref, q_ref, *refs):
    sources = []
    for count, *_ in kinds:
        sources.append((refs[0], refs[1 : 1 + count]))
        refs = refs[1 + count :]
    if not first:
        acc_in, stat_in = refs[:2]
        refs = refs[2:]
    if onto:
        refs = refs[1:]
    if last:
        out_ref, bias_ref, class_ref, turned_ref = refs
    else:
        acc_out, stat_out, bias_ref, class_ref, turned_ref = refs
    tokens = q_ref.shape[0]
    sizes = [key_ref.shape[0] for key_ref, _ in sources]
    position = lax.axis_index("frame")

    @pl.when(pl.program_id(0) == 0)
    def _():
        row = lax.broadcasted_iota(jnp.int32, (tokens, HD), 0) // COLS
        lane = lax.broadcasted_iota(jnp.int32, (tokens, HD), 1)
        bias = jnp.zeros((tokens, HD), jnp.float32)
        base, start = 0, 0
        for (_, windowed, there, _), size in zip(kinds, sizes):
            there = there(position)
            if windowed:
                wide = size // COLS
                here = jnp.abs(row - (lane - base)) <= jnp.where(there, window_ref[0], -1)
                hot = row[:size] == lane[:size] - base
            else:
                wide = 1
                here = lane * 0 + jnp.where(there, 1, 0) > 0
                hot = lane[:size] == base
            mine = (lane >= base) & (lane < base + wide)
            bias = jnp.where(mine & ~here, MASKED, bias)
            class_ref[pl.ds(start, size), :] = jnp.where(hot, 1.0, 0.0).astype(jnp.bfloat16)
            base, start = base + wide, start + size
        bias_ref[...] = bias.astype(jnp.bfloat16)
        turned_ref[:, pl.ds(HD, ONES), :] = jnp.ones((together, ONES, sum(sizes)), jnp.bfloat16)

    def column(head):
        return pl.ds(head * HD, HD)

    def scores_of(head):
        keys = jnp.concatenate([key_ref[:, column(head)] for key_ref, _ in sources], axis=0)
        keys = jnp.concatenate([keys, class_ref[...]], axis=1)
        query = jnp.concatenate([q_ref[:, column(head)], bias_ref[...]], axis=1)
        scores = lax.dot_general(
            keys, query, (((1,), (1,)), ((), ())), preferred_element_type=jnp.float32
        )
        return scores, jnp.max(scores, axis=0, keepdims=True)

    for head in range(together):
        start = 0
        for (_, value_refs), (*_, parted), size in zip(sources, kinds, sizes):

            def put(value, start):
                turned_ref[head, pl.ds(0, HD), pl.ds(start, value.shape[0])] = value.T

            if parted is None:
                put(value_refs[0][:, column(head)], start)
            else:
                reader_of, choose = parted
                reader, which = reader_of(position)
                pick = picks_ref[which, jnp.clip(reader, 0, picks_ref.shape[1] - 1)]
                others = value_refs[1][:, column(head)]
                if value_refs[2:]:
                    others = jnp.where(choose(position), value_refs[2][:, column(head)], others)
                put(value_refs[0][:, column(head)], pl.multiple_of(start + pick * SUB, SUB))
                for other in range(size // SUB - 1):
                    block = other + jnp.where(other >= pick, 1, 0)
                    part = others[other * SUB : (other + 1) * SUB]
                    put(part, pl.multiple_of(start + block * SUB, SUB))
            start += size
    upcoming = scores_of(0)
    for head in range(together):
        scores, peak = upcoming
        if head + 1 < together:
            upcoming = scores_of(head + 1)
        if not first:
            before = stat_in[8 * head : 8 * head + 1, :]
            peak = jnp.maximum(peak, before)
        weights = jnp.exp2((scores - peak) * BASE2).astype(jnp.bfloat16)
        total = jnp.dot(turned_ref[head], weights, preferred_element_type=jnp.float32)
        acc, norm = total[:HD, :], total[HD : HD + 1, :]
        if not first:
            scale = jnp.exp2((before - peak) * BASE2)
            acc = acc + acc_in[column(head), :] * scale
            norm = norm + stat_in[8 * head + 1 : 8 * head + 2, :] * scale
        if last:
            out_ref[:, column(head)] = (acc / norm).T.astype(out_ref.dtype)
        else:
            acc_out[column(head), :] = acc
            stat_out[8 * head : 8 * head + 1, :] = peak
            stat_out[8 * head + 1 : 8 * head + 2, :] = norm


def attend(window, picks, query, sources, state, last, part=None, target=None):
    tokens, width = query.shape
    first_head, heads = part or (0, width // HD)
    together = next(n for n in (3, 2, 1) if heads % n == 0 and first_head % n == 0)
    kinds = tuple((len(source[2]), *source[4:]) for source in sources)

    def columns(rows, base):
        return pl.BlockSpec((rows, HD * together), lambda h, window: (0, base // together + h))

    specs = [pl.BlockSpec(memory_space=pltpu.SMEM), columns(tokens, first_head)]
    operands = [picks.T, query]
    keys_count = 0
    for key, key_base, values, value_bases, *_ in sources:
        specs.append(columns(key.shape[0], key_base))
        specs += [columns(value.shape[0], base) for value, base in zip(values, value_bases)]
        operands += [key, *values]
        keys_count += key.shape[0]
    base = first_head // together
    state_specs = [
        pl.BlockSpec((HD * together, tokens), lambda h, window: (base + h, 0)),
        pl.BlockSpec((8 * together, tokens), lambda h, window: (base + h, 0)),
    ]
    moved_bytes = 2 * (tokens + 2 * keys_count) * heads * HD
    aliases = {}
    if state is not None:
        if not last:
            aliases = {1 + len(operands): 0, 2 + len(operands): 1}
        specs += state_specs
        operands += list(state)
        moved_bytes += 4 * tokens * heads * HD
    if target is not None:
        aliases = {1 + len(operands): 0}
        specs.append(pl.BlockSpec(memory_space=pl.ANY))
        operands.append(target)
    if last:
        out_shape = jax.ShapeDtypeStruct((tokens, width), jnp.bfloat16)
        out_specs = columns(tokens, first_head)
    else:
        out_shape = [
            jax.ShapeDtypeStruct((width, tokens), jnp.float32),
            jax.ShapeDtypeStruct((width // HD * 8, tokens), jnp.float32),
        ]
        out_specs = state_specs
    return pl.pallas_call(
        functools.partial(
            attend_kernel, kinds, together, state is None, last, target is not None
        ),
        out_shape=out_shape,
        grid_spec=pltpu.PrefetchScalarGridSpec(
            num_scalar_prefetch=1,
            grid=(heads // together,),
            in_specs=specs,
            out_specs=out_specs,
            scratch_shapes=[
                pltpu.VMEM((tokens, HD), jnp.bfloat16),
                pltpu.VMEM((keys_count, HD), jnp.bfloat16),
                pltpu.VMEM((together, HD + ONES, keys_count), jnp.bfloat16),
            ],
        ),
        input_output_aliases=aliases,
        compiler_params=pltpu.CompilerParams(vmem_limit_bytes=67_043_328),
        cost_estimate=pl.CostEstimate(
            flops=4 * tokens * keys_count * heads * HD,
            bytes_accessed=moved_bytes + 2 * tokens * heads * HD,
            transcendentals=tokens * keys_count * heads,
        ),
    )(window, *operands)


def body(query_in, keys_in, values_in, far_picks, win_rows):
    frames = lax.axis_size("frame")
    query, keys, values = query_in[0], keys_in[0], values_in[0]
    heads = query.shape[1] // HD
    offsets = offsets_for(frames)
    shared = frames % 2 == 0 and 2 in offsets

    def beyond_of(position):
        return position + 2 * (position % 2) - 1

    def there(frame):
        return (frame >= 0) & (frame < frames)

    outward = [(1, is_odd), (-1, is_even)]
    inward = [(1, is_even), (-1, is_odd)]
    hop = [(-2, lambda f: f % 4 == 3 and f + 1 < frames), (2, lambda f: f % 4 == 0 and f > 0)]
    skip = [(3, lambda f: f % 4 == 1), (-3, lambda f: f % 4 == 2)]

    def turning(position):
        return (position + 1) % 4 < 2

    straight = [(1, lambda f: f % 4 == 1), (-1, lambda f: f % 4 == 2)]
    beyond_keys = moved(keys, outward)
    half = heads // 2
    halves = [(0, half), (half, heads - half)]

    far = []
    for column in sorted(range(len(offsets)), key=lambda c: -abs(offsets[c])):
        offset = offsets[column]
        if shared and abs(offset) == 2:
            continue
        if 2 * abs(offset) == frames:
            if offset > 0:
                continue
            back, ahead = column, offsets.index(-offset)
            half = -offset

            def across(position, half=half, back=back, ahead=ahead):
                low = position < half
                return position + jnp.where(low, half, -half), jnp.where(low, back, ahead)

            steps = [(half, lambda f, half=half: f < half), (-half, lambda f, half=half: f >= half)]
            far.append((steps, across, lambda position: position >= 0))
            continue
        far.append(
            (
                [(-offset, anyone)],
                lambda position, offset=offset, column=column: (position - offset, column),
                lambda position, offset=offset: there(position + offset),
            )
        )
    if shared:
        back, ahead = offsets.index(-2), offsets.index(2)

        def beyond_reader(position):
            odd = position % 2
            return position - 2 + 4 * odd, jnp.where(odd == 0, ahead, back)

        def past(position):
            odd = position % 2
            return position - 1 + 2 * odd, jnp.where(odd == 0, ahead, back)

        def two_back(position):
            return there(position - 2 + 4 * (position % 2))

        def partner(position):
            odd = position % 2
            return position + 1 - 2 * odd, jnp.where(odd == 0, back, ahead)

    readers = [reader for _, reader, _ in far]
    parts = [(start * HD, number * HD) for start, number in halves]
    if shared:
        *blocks, picked, lower, upper = gather(
            far_picks, [keys, values], [*readers, beyond_reader], frames, tuple(parts)
        )
    else:
        blocks = gather(far_picks, [keys, values], readers, frames)
        lower, upper = [values[:, start : start + width] for start, width in parts]
    around = []
    if shared:
        picked = moved(picked, outward)
        around = [moved(lower, hop)]
    lower = moved(lower, straight if shared else outward)
    upper = moved(upper, outward)
    arrived = []
    for block, (steps, _, _) in zip(blocks, far):
        arrived.append(moved(block, steps))
    mate_keys = moved(keys, inward)
    mate_values = moved(values, inward)

    if shared:
        (behind,) = gather(far_picks, [mate_keys, mate_values], [past], frames)
        behind = moved(behind, outward)
        around = [moved(around[0], skip)]

    def always(position):
        return position >= 0

    def near_there(position):
        return there(beyond_of(position))

    def ahead_there(position):
        return there(position + 2 - 4 * (position % 2))

    own = [
        (keys, 0, [values], [0], True, always, None),
        (mate_keys, 0, [mate_values], [0], True, always, None),
    ]
    state = attend(win_rows, far_picks, query, own, None, False)
    distant = [
        (block, 0, [block], [heads], False, there, None)
        for block, (_, _, there) in zip(arrived, far)
    ]
    if not shared:
        for part, values in ((halves[0], lower), (halves[1], upper)):
            nearby = [(beyond_keys, part[0], [values], [0], True, near_there, None)]
            state = attend(win_rows, far_picks, query, nearby, state, False, part)
        return attend(win_rows, far_picks, query, distant, state, True)[None]
    (handed_keys,) = gather(far_picks, [beyond_keys], [partner], frames)
    handed_values = moved(picked, inward)
    handed_keys = moved(handed_keys, inward)
    distant.append((handed_keys, 0, [handed_values], [0], False, ahead_there, None))
    state = attend(win_rows, far_picks, query, distant, state, False)
    out = None
    for part, values in ((halves[0], [lower, *around]), (halves[1], [upper])):
        start = part[0]
        nearby = [
            (
                beyond_keys,
                start,
                [picked, *values],
                [start] + [0] * len(values),
                True,
                near_there,
                (partner, turning),
            ),
            (behind, start, [behind], [heads + start], False, two_back, None),
        ]
        out = attend(win_rows, far_picks, query, nearby, state, True, part, out)
    return out[None]


def solution(mesh):
    in_specs = (
        P(("groups", "frame"), None, None),
        P(("groups", "frame"), None, None),
        P(("groups", "frame"), None, None),
        P("groups", None),
        P(("groups", "frame")),
    )
    out_specs = P(("groups", "frame"), None, None)

    return jax.shard_map(body, mesh=mesh, in_specs=in_specs, out_specs=out_specs, check_vma=False)
```

```python
import functools
import math

import jax
import jax.numpy as jnp
from jax import lax
from jax.experimental import pallas as pl
from jax.experimental.pallas import tpu as pltpu
from jax.sharding import PartitionSpec as P

HD = 128
COLS = 32
SUB = 128
NREACH = 3
MASKED = -1e30
BASE2 = math.log2(math.e) / math.sqrt(HD)
ONES = 16


def offsets_for(frames):
    spacing = [frames // 2 ** (NREACH - level_index) for level_index in range(NREACH)]
    return [-stride for stride in spacing] + [stride for stride in spacing]


def moved(value, steps):
    count = lax.axis_size("frame")
    pairs = [(f, f + step) for step, who in steps for f in range(count) if who(f)]
    pairs = [(source, target) for source, target in pairs if 0 <= target < count]
    return lax.ppermute(value, "frame", pairs)


def anyone(frame):
    return True


def is_even(frame):
    return frame % 2 == 0


def is_odd(frame):
    return frame % 2 == 1


def gather_kernel(readers, frames, count, parts, picks_ref, *refs):
    arrays, outs = refs[:count], refs[count:-1]
    sems = refs[-1]
    position = lax.axis_index("frame")
    copies = []

    def copy(source, target):
        copies.append(pltpu.make_async_copy(source, target, sems.at[len(copies)]))

    def block(pick):
        return pl.ds(pl.multiple_of(pick * SUB, SUB), SUB)

    def pick_of(reader_of):
        reader, column = reader_of(position)
        return picks_ref[column, jnp.clip(reader, 0, frames - 1)]

    for reader_of, out in zip(readers[:-1] if parts else readers, outs):
        rows = block(pick_of(reader_of))
        start = 0
        for source in arrays:
            copy(source.at[rows, :], out.at[:, pl.ds(start, source.shape[1])])
            start += source.shape[1]
    if parts:
        pick, source = pick_of(readers[-1]), arrays[-1]
        outs = outs[len(readers) - 1 :]
        copy(source.at[block(pick), :], outs[0])
        for (start, width), out in zip(parts, outs[1:]):
            for other in range(source.shape[0] // SUB - 1):
                rows = block(other + jnp.where(other >= pick, 1, 0))
                target = out.at[pl.ds(other * SUB, SUB), :]
                copy(source.at[rows, pl.ds(start, width)], target)
    for each in copies:
        each.start()
    for each in copies:
        each.wait()


def gather(picks, arrays, readers, frames, parts=()):
    width = sum(array.shape[1] for array in arrays)
    dtype = arrays[0].dtype
    shapes = [(SUB, width)] * (len(readers) - bool(parts))
    count = len(shapes) * len(arrays)
    if parts:
        tokens, last_width = arrays[-1].shape
        shapes += [(SUB, last_width)] + [(tokens - SUB, width) for _, width in parts]
        count += 1 + (tokens // SUB - 1) * len(parts)
    return pl.pallas_call(
        functools.partial(gather_kernel, readers, frames, len(arrays), parts),
        out_shape=[jax.ShapeDtypeStruct(shape, dtype) for shape in shapes],
        in_specs=[
            pl.BlockSpec(memory_space=pltpu.SMEM),
            *[pl.BlockSpec(memory_space=pltpu.HBM)] * len(arrays),
        ],
        out_specs=[pl.BlockSpec(memory_space=pltpu.VMEM) for _ in shapes],
        scratch_shapes=[pltpu.SemaphoreType.DMA((count,))],
        compiler_params=pltpu.CompilerParams(vmem_limit_bytes=67_043_328),
        cost_estimate=pl.CostEstimate(
            flops=0,
            bytes_accessed=4 * sum(rows * columns for rows, columns in shapes),
            transcendentals=0,
        ),
    )(picks.T, *arrays)


def attend_kernel(kinds, together, first, last, onto, window_ref, picks_ref, q_ref, *refs):
    sources = []
    for count, *_ in kinds:
        sources.append((refs[0], refs[1 : 1 + count]))
        refs = refs[1 + count :]
    if not first:
        acc_in, stat_in = refs[:2]
        refs = refs[2:]
    if onto:
        refs = refs[1:]
    if last:
        out_ref, bias_ref, class_ref, turned_ref = refs
    else:
        acc_out, stat_out, bias_ref, class_ref, turned_ref = refs
    tokens = q_ref.shape[0]
    sizes = [key_ref.shape[0] for key_ref, _ in sources]
    position = lax.axis_index("frame")

    @pl.when(pl.program_id(0) == 0)
    def _():
        row = lax.broadcasted_iota(jnp.int32, (tokens, HD), 0) // COLS
        lane = lax.broadcasted_iota(jnp.int32, (tokens, HD), 1)
        bias = jnp.zeros((tokens, HD), jnp.float32)
        base, start = 0, 0
        for (_, windowed, there, _), size in zip(kinds, sizes):
            there = there(position)
            if windowed:
                wide = size // COLS
                here = jnp.abs(row - (lane - base)) <= jnp.where(there, window_ref[0], -1)
                hot = row[:size] == lane[:size] - base
            else:
                wide = 1
                here = lane * 0 + jnp.where(there, 1, 0) > 0
                hot = lane[:size] == base
            mine = (lane >= base) & (lane < base + wide)
            bias = jnp.where(mine & ~here, MASKED, bias)
            class_ref[pl.ds(start, size), :] = jnp.where(hot, 1.0, 0.0).astype(jnp.bfloat16)
            base, start = base + wide, start + size
        bias_ref[...] = bias.astype(jnp.bfloat16)
        turned_ref[:, pl.ds(HD, ONES), :] = jnp.ones((together, ONES, sum(sizes)), jnp.bfloat16)

    def column(head):
        return pl.ds(head * HD, HD)

    def scores_of(head):
        keys = jnp.concatenate([key_ref[:, column(head)] for key_ref, _ in sources], axis=0)
        keys = jnp.concatenate([keys, class_ref[...]], axis=1)
        query = jnp.concatenate([q_ref[:, column(head)], bias_ref[...]], axis=1)
        scores = lax.dot_general(
            keys, query, (((1,), (1,)), ((), ())), preferred_element_type=jnp.float32
        )
        return scores, jnp.max(scores, axis=0, keepdims=True)

    for head in range(together):
        start = 0
        for (_, value_refs), (*_, parted), size in zip(sources, kinds, sizes):

            def put(value, start):
                turned_ref[head, pl.ds(0, HD), pl.ds(start, value.shape[0])] = value.T

            if parted is None:
                put(value_refs[0][:, column(head)], start)
            else:
                reader_of, choose = parted
                reader, which = reader_of(position)
                pick = picks_ref[which, jnp.clip(reader, 0, picks_ref.shape[1] - 1)]
                others = value_refs[1][:, column(head)]
                if value_refs[2:]:
                    others = jnp.where(choose(position), value_refs[2][:, column(head)], others)
                put(value_refs[0][:, column(head)], pl.multiple_of(start + pick * SUB, SUB))
                for other in range(size // SUB - 1):
                    block = other + jnp.where(other >= pick, 1, 0)
                    part = others[other * SUB : (other + 1) * SUB]
                    put(part, pl.multiple_of(start + block * SUB, SUB))
            start += size
    upcoming = scores_of(0)
    for head in range(together):
        scores, peak = upcoming
        if head + 1 < together:
            upcoming = scores_of(head + 1)
        if not first:
            before = stat_in[8 * head : 8 * head + 1, :]
            peak = jnp.maximum(peak, before)
        weights = jnp.exp2((scores - peak) * BASE2).astype(jnp.bfloat16)
        total = jnp.dot(turned_ref[head], weights, preferred_element_type=jnp.float32)
        acc, norm = total[:HD, :], total[HD : HD + 1, :]
        if not first:
            scale = jnp.exp2((before - peak) * BASE2)
            acc = acc + acc_in[column(head), :] * scale
            norm = norm + stat_in[8 * head + 1 : 8 * head + 2, :] * scale
        if last:
            out_ref[:, column(head)] = (acc / norm).T.astype(out_ref.dtype)
        else:
            acc_out[column(head), :] = acc
            stat_out[8 * head : 8 * head + 1, :] = peak
            stat_out[8 * head + 1 : 8 * head + 2, :] = norm


def attend(window, picks, query, sources, state, last, part=None, target=None):
    tokens, width = query.shape
    first_head, heads = part or (0, width // HD)
    together = next(n for n in (3, 2, 1) if heads % n == 0 and first_head % n == 0)
    kinds = tuple((len(source[2]), *source[4:]) for source in sources)

    def columns(rows, base):
        return pl.BlockSpec((rows, HD * together), lambda h, window: (0, base // together + h))

    specs = [pl.BlockSpec(memory_space=pltpu.SMEM), columns(tokens, first_head)]
    operands = [picks.T, query]
    keys_count = 0
    for key, key_base, values, value_bases, *_ in sources:
        specs.append(columns(key.shape[0], key_base))
        specs += [columns(value.shape[0], base) for value, base in zip(values, value_bases)]
        operands += [key, *values]
        keys_count += key.shape[0]
    base = first_head // together
    state_specs = [
        pl.BlockSpec((HD * together, tokens), lambda h, window: (base + h, 0)),
        pl.BlockSpec((8 * together, tokens), lambda h, window: (base + h, 0)),
    ]
    moved_bytes = 2 * (tokens + 2 * keys_count) * heads * HD
    aliases = {}
    if state is not None:
        if not last:
            aliases = {1 + len(operands): 0, 2 + len(operands): 1}
        specs += state_specs
        operands += list(state)
        moved_bytes += 4 * tokens * heads * HD
    if target is not None:
        aliases = {1 + len(operands): 0}
        specs.append(pl.BlockSpec(memory_space=pl.ANY))
        operands.append(target)
    if last:
        out_shape = jax.ShapeDtypeStruct((tokens, width), jnp.bfloat16)
        out_specs = columns(tokens, first_head)
    else:
        out_shape = [
            jax.ShapeDtypeStruct((width, tokens), jnp.float32),
            jax.ShapeDtypeStruct((width // HD * 8, tokens), jnp.float32),
        ]
        out_specs = state_specs
    return pl.pallas_call(
        functools.partial(
            attend_kernel, kinds, together, state is None, last, target is not None
        ),
        out_shape=out_shape,
        grid_spec=pltpu.PrefetchScalarGridSpec(
            num_scalar_prefetch=1,
            grid=(heads // together,),
            in_specs=specs,
            out_specs=out_specs,
            scratch_shapes=[
                pltpu.VMEM((tokens, HD), jnp.bfloat16),
                pltpu.VMEM((keys_count, HD), jnp.bfloat16),
                pltpu.VMEM((together, HD + ONES, keys_count), jnp.bfloat16),
            ],
        ),
        input_output_aliases=aliases,
        compiler_params=pltpu.CompilerParams(vmem_limit_bytes=67_043_328),
        cost_estimate=pl.CostEstimate(
            flops=4 * tokens * keys_count * heads * HD,
            bytes_accessed=moved_bytes + 2 * tokens * heads * HD,
            transcendentals=tokens * keys_count * heads,
        ),
    )(window, *operands)


def body(query_in, keys_in, values_in, far_picks, win_rows):
    frames = lax.axis_size("frame")
    query, keys, values = query_in[0], keys_in[0], values_in[0]
    heads = query.shape[1] // HD
    offsets = offsets_for(frames)
    shared = frames % 2 == 0 and 2 in offsets

    def beyond_of(position):
        return position + 2 * (position % 2) - 1

    def there(frame):
        return (frame >= 0) & (frame < frames)

    outward = [(1, is_odd), (-1, is_even)]
    inward = [(1, is_even), (-1, is_odd)]
    middle = (frames // 4 - 1) // 2

    def up(f, half):
        return (f % 4 == 3) & (f + 1 < frames) & (f // 4 + half <= middle)

    def down(f, half):
        return (f % 4 == 0) & (f > 0) & (f // 4 - 1 - half >= middle)

    def hop(half):
        return [(-2, lambda f: up(f, half)), (2, lambda f: down(f, half))]

    def skip(half):
        return [(3, lambda f: up(f + 2, half)), (-3, lambda f: down(f - 2, half))]

    def straight(half):
        ahead = (1, lambda f: (f % 2 == 1) & (not up(f, half)))
        return [ahead, (-1, lambda f: (f % 2 == 0) & (not down(f, half)))]

    def turning(half):
        return lambda position: up(position - 1, half) | down(position + 1, half)

    beyond_keys = moved(keys, outward)
    half = heads // 2
    halves = [(0, half), (half, heads - half)]

    far = []
    for column in sorted(range(len(offsets)), key=lambda c: -abs(offsets[c])):
        offset = offsets[column]
        if shared and abs(offset) == 2:
            continue
        if 2 * abs(offset) == frames:
            if offset > 0:
                continue
            back, ahead = column, offsets.index(-offset)
            half = -offset

            def across(position, half=half, back=back, ahead=ahead):
                low = position < half
                return position + jnp.where(low, half, -half), jnp.where(low, back, ahead)

            steps = [(half, lambda f, half=half: f < half), (-half, lambda f, half=half: f >= half)]
            far.append((steps, across, lambda position: position >= 0))
            continue
        far.append(
            (
                [(-offset, anyone)],
                lambda position, offset=offset, column=column: (position - offset, column),
                lambda position, offset=offset: there(position + offset),
            )
        )
    if shared:
        back, ahead = offsets.index(-2), offsets.index(2)

        def beyond_reader(position):
            odd = position % 2
            return position - 2 + 4 * odd, jnp.where(odd == 0, ahead, back)

        def past(position):
            odd = position % 2
            return position - 1 + 2 * odd, jnp.where(odd == 0, ahead, back)

        def two_back(position):
            return there(position - 2 + 4 * (position % 2))

        def partner(position):
            odd = position % 2
            return position + 1 - 2 * odd, jnp.where(odd == 0, back, ahead)

    readers = [reader for _, reader, _ in far]
    parts = [(start * HD, number * HD) for start, number in halves]
    if shared:
        *blocks, picked, lower, upper = gather(
            far_picks, [keys, values], [*readers, beyond_reader], frames, tuple(parts)
        )
    else:
        blocks = gather(far_picks, [keys, values], readers, frames)
        lower, upper = [values[:, start : start + width] for start, width in parts]
    around = []
    if shared:
        picked = moved(picked, outward)
        around = [moved(lower, hop(0))]
        around.append(moved(upper, hop(1)))
    lower = moved(lower, straight(0) if shared else outward)
    upper = moved(upper, straight(1) if shared else outward)
    arrived = []
    for block, (steps, _, _) in zip(blocks, far):
        arrived.append(moved(block, steps))
    mate_keys = moved(keys, inward)
    mate_values = moved(values, inward)

    if shared:
        (behind,) = gather(far_picks, [mate_keys, mate_values], [past], frames)
        behind = moved(behind, outward)
        lower_around = moved(around[0], skip(0))
        upper_around = moved(around[1], skip(1))

    def always(position):
        return position >= 0

    def near_there(position):
        return there(beyond_of(position))

    def ahead_there(position):
        return there(position + 2 - 4 * (position % 2))

    own = [
        (keys, 0, [values], [0], True, always, None),
        (mate_keys, 0, [mate_values], [0], True, always, None),
    ]
    state = attend(win_rows, far_picks, query, own, None, False)
    distant = [
        (block, 0, [block], [heads], False, there, None)
        for block, (_, _, there) in zip(arrived, far)
    ]
    if not shared:
        for part, values in ((halves[0], lower), (halves[1], upper)):
            nearby = [(beyond_keys, part[0], [values], [0], True, near_there, None)]
            state = attend(win_rows, far_picks, query, nearby, state, False, part)
        return attend(win_rows, far_picks, query, distant, state, True)[None]
    (handed_keys,) = gather(far_picks, [beyond_keys], [partner], frames)
    handed_values = moved(picked, inward)
    handed_keys = moved(handed_keys, inward)
    distant.append((handed_keys, 0, [handed_values], [0], False, ahead_there, None))
    state = attend(win_rows, far_picks, query, distant, state, False)
    out = None
    for which, part, values in ((0, halves[0], [lower, lower_around]), (1, halves[1], [upper, upper_around])):
        start = part[0]
        nearby = [
            (
                beyond_keys,
                start,
                [picked, *values],
                [start] + [0] * len(values),
                True,
                near_there,
                (partner, turning(which)),
            ),
            (behind, start, [behind], [heads + start], False, two_back, None),
        ]
        out = attend(win_rows, far_picks, query, nearby, state, True, part, out)
    return out[None]


def solution(mesh):
    in_specs = (
        P(("groups", "frame"), None, None),
        P(("groups", "frame"), None, None),
        P(("groups", "frame"), None, None),
        P("groups", None),
        P(("groups", "frame")),
    )
    out_specs = P(("groups", "frame"), None, None)

    return jax.shard_map(body, mesh=mesh, in_specs=in_specs, out_specs=out_specs, check_vma=False)
```
